256 devices in a mesh: wide: 32 (over z_lo, x, core), narrow: 8 (over z_hi, y).
Axes of the slice: x: 4, y: 4, z: 8 (z_hi: 2, z_lo: 4; z = z_hi * 4 + z_lo), core: 2. Of those that a mesh axis runs over, the one named last changes fastest.
Arguments:
- krylov: float32 [2, 134217728], P(None, ('wide', 'narrow')), may hold values from -6 to 6
- fitness_class: int32 [4194304], P(('wide', 'narrow')), may hold values from 0 to 7
- rate_index: int32 [2], replicated, may hold values from 4 to 15
Outputs:
- images: float32 [2, 134217728], P(None, ('wide', 'narrow'))
The draws below stay inside these ranges and needn't reach their ends.
All inputs are finite; a program needn't handle non-finite values.
Results may differ from the reference program's by a relative error of at most 0.00014.
Values sent between devices are 32-bit elements; how exact they have to be, the bound alone decides.
No kernel may reach another device: no remote copies, remote signals or barrier semaphores. Data moves between devices by JAX's collectives and lax.ppermute only.
A program may use at most 128 MiB of HBM per device.

```python
import jax
import jax.numpy as jnp
from jax import lax

FBLOCK = 32
ITERS = 2
GENOTYPES = 134217728


def touch_ends(result, own_key, smallest, top_value):
    index_at = [jax.random.randint(jax.random.fold_in(own_key, axis), (), 0, length) for axis, length in enumerate(result.shape)]
    longest = result.shape.index(max(result.shape))
    beside = index_at[:longest] + [(index_at[longest] + 1) % result.shape[longest]] + index_at[longest + 1:]
    return result.at[tuple(index_at)].set(smallest).at[tuple(beside)].set(top_value)


def block_scale(rng, dims, cuts, least, top_value):
    factor_of = 1.0
    for axis_at, shards_of in cuts:
        heights = jax.random.uniform(jax.random.fold_in(jax.random.fold_in(rng, 6), axis_at), (shards_of,), jnp.float32, least / len(cuts), top_value / len(cuts))
        factor_of = factor_of * jnp.repeat(jnp.exp(heights), dims[axis_at] // shards_of).reshape((-1,) + (1,) * (len(dims) - 1 - axis_at))
    return factor_of


def bell_draw(rng, dims, spread, most, split=(), kind=jnp.bfloat16):
    result = spread * jax.random.normal(rng, dims, jnp.float32)
    if split:
        result = result * block_scale(rng, dims, split, -0.22, 0.18)
    return jnp.clip(result, -most, most).astype(kind)


def setup_inputs(seed: int = 0) -> dict:
    arg_keys = jax.random.split(jax.random.key(seed), 4)
    krylov = bell_draw(arg_keys[0], (2, GENOTYPES), 1.0, 6.0, ((1, 256),), jnp.float32)
    fitness_class = touch_ends(jax.random.randint(arg_keys[1], (GENOTYPES // FBLOCK,), 0, 8), jax.random.fold_in(arg_keys[1], 1), 0, 7).astype(jnp.int32)
    rate_index = jax.random.randint(arg_keys[2], (2,), 4, 16).astype(jnp.int32)
    return {"krylov": krylov, "fitness_class": fitness_class, "rate_index": rate_index}


def mutation_rates(rate_index, total_bits):
    levels = 0.004 * (rate_index.astype(jnp.float32) + 1.0)
    position = jnp.arange(total_bits, dtype=jnp.float32)
    profile = 1.0 + 0.5 * jnp.cos(2.0 * position)
    return levels[:, None] * profile[None, :]


def kronecker(mutation, first_site, width_bits):
    middle = 1 << width_bits
    indices = jnp.arange(middle, dtype=jnp.int32)
    product = jnp.ones((mutation.shape[0], middle, middle), jnp.float32)
    for bit_pos in range(width_bits):
        column = (indices >> bit_pos) & 1
        agreeing = column[:, None] == column[None, :]
        chance = mutation[:, first_site + bit_pos][:, None, None]
        product = product * jnp.where(agreeing[None], 1.0 - chance, chance)
    return product


def split_widths(amount):
    groups = -(-amount // 7)
    common = amount // groups
    leftover = amount % groups
    return [common + 1 if number < leftover else common for number in range(groups)]


def mix_range(vectors, mutation, first_pos, amount, site_shift):
    vector_count, length = vectors.shape
    offset = first_pos
    for group_width in split_widths(amount):
        low_size = 1 << offset
        middle = 1 << group_width
        high_size = length // (low_size * middle)
        matrix = kronecker(mutation, offset + site_shift, group_width)
        if low_size == 1:
            shaped = vectors.reshape(vector_count, high_size, middle)
            mixed_out = jnp.einsum("aij,ahj->ahi", matrix, shaped, precision=lax.Precision.HIGHEST)
        else:
            shaped = vectors.reshape(vector_count, high_size, middle, low_size)
            mixed_out = jnp.einsum("aij,ahjl->ahil", matrix, shaped, precision=lax.Precision.HIGHEST)
        vectors = mixed_out.reshape(vector_count, length)
        offset = offset + group_width
    return vectors


def apply_fitness(vectors, classes):
    vector_count, length = vectors.shape
    blocks = classes.shape[0]
    scale_row = 0.5 + 0.25 * classes.astype(jnp.float32)
    shaped = vectors.reshape(vector_count, blocks, length // blocks) * scale_row[None, :, None]
    return shaped.reshape(vector_count, length)


def reference(krylov, fitness_class, rate_index):
    length = krylov.shape[1]
    total_bits = length.bit_length() - 1
    mutation = mutation_rates(rate_index, total_bits)
    vectors = krylov
    for iteration in range(ITERS):
        vectors = apply_fitness(vectors, fitness_class)
        vectors = mix_range(vectors, mutation, 0, total_bits, 0)
    return vectors
```

```python
import jax
import jax.numpy as jnp
import numpy as np
from jax import lax
from jax.experimental import pallas as pl
from jax.experimental.pallas import tpu as pltpu
from jax.sharding import PartitionSpec as P

AXES = ("wide", "narrow")
DEVICES = 256
SITES = 27
LOCAL_ROWS = 4096
PEER_ROWS = LOCAL_ROWS // DEVICES
PROFILE = [float(1.0 + 0.5 * np.cos(2.0 * site)) for site in range(SITES)]
F32 = jnp.float32
BF16 = jnp.bfloat16


def chances(rate_ref, vector):
    level = 0.004 * (rate_ref[vector].astype(F32) + 1.0)
    return [level * PROFILE[site] for site in range(SITES)]


def mix_bits(tiles, chance_of_bit):
    tiles = list(tiles)
    for bit, chance in enumerate(chance_of_bit):
        step = 1 << bit
        for low in range(len(tiles)):
            if low & step:
                continue
            flow = chance * (tiles[low | step] - tiles[low])
            tiles[low] = tiles[low] + flow
            tiles[low | step] = tiles[low | step] - flow
    return tiles


def lane_matrix(chance):
    row = lax.broadcasted_iota(jnp.int32, (128, 128), 0)
    column = lax.broadcasted_iota(jnp.int32, (128, 128), 1)
    differ = row ^ column
    product = jnp.ones((128, 128), F32)
    for site in range(7):
        product = product * jnp.where((differ >> site) & 1 == 0, 1.0 - chance[site], chance[site])
    high = product.astype(BF16)
    low = (product - high.astype(F32)).astype(BF16)
    top = jnp.concatenate([high, low], axis=1)
    bottom = jnp.concatenate([high, jnp.zeros_like(low)], axis=1)
    return jnp.concatenate([top, bottom], axis=0)


def mix_lanes(tiles, matrix):
    rows = jnp.concatenate(tiles, axis=0)
    high = rows.astype(BF16)
    low = (rows - high.astype(F32)).astype(BF16)
    both = jnp.dot(jnp.concatenate([high, low], axis=1), matrix, preferred_element_type=F32)
    mixed = both[:, :128] + both[:, 128:]
    return [mixed[8 * at : 8 * at + 8] for at in range(len(tiles))]


def mix_sublanes(tiles, chance):
    sub = lax.broadcasted_iota(jnp.int32, (8, 128), 0)
    mixed = []
    for tile in tiles:
        for bit in range(3):
            step = 1 << bit
            if step == 4:
                partner = pltpu.roll(tile, 4, 0)
            else:
                partner = jnp.where(
                    sub & step == 0, pltpu.roll(tile, 8 - step, 0), pltpu.roll(tile, step, 0)
                )
            tile = tile + chance[bit] * (partner - tile)
        mixed.append(tile)
    return mixed


def spread_fitness(row, count):
    sub = lax.broadcasted_iota(jnp.int32, (8, 128), 0)
    lane = lax.broadcasted_iota(jnp.int32, (8, 128), 1)
    source = jnp.broadcast_to(row, (8, 128))
    return [
        jnp.take_along_axis(source, 4 * (8 * at + sub) + (lane >> 5), axis=1, mode="promise_in_bounds")
        for at in range(count)
    ]


def first_kernel(vector, rate_ref, class_ref, x_ref, out_ref):
    step = pl.program_id(0)
    chance = chances(rate_ref, vector)
    fitness = 0.5 + 0.25 * class_ref[...].astype(F32)
    tiles = []
    for group in range(8):
        for at, scale in enumerate(spread_fitness(fitness[group : group + 1], 4)):
            start = group * 64 + at * 16 + vector
            tiles.append(x_ref[pl.ds(start, 8, stride=2), :] * scale)
    tiles = mix_lanes(tiles, lane_matrix(chance))
    tiles = mix_sublanes(tiles, chance[7:10])
    tiles = mix_bits(tiles, chance[10:15])
    for at, tile in enumerate(tiles):
        out_ref[pl.ds(pl.multiple_of(step * 256, 256) + 8 * at, 8), :] = tile

    @pl.when(step == pl.num_programs(0) - 1)
    def _():
        @pl.loop(0, 32)
        def _(at):
            places = [pl.ds(pl.multiple_of(256 * top + 8 * at, 8), 8) for top in range(16)]
            mixed = mix_bits([out_ref[place, :] for place in places], chance[15:19])
            for place, tile in zip(places, mixed):
                out_ref[place, :] = tile


def mix_low_devices(source_ref, target_ref, chance):
    @pl.loop(0, 32)
    def _(at):
        high = at // 2
        rows = pl.ds(pl.multiple_of(8 * (at % 2), 8), 8)
        mixed = mix_bits([source_ref[high * 16 + low, rows, :] for low in range(16)], chance)
        for low, tile in enumerate(mixed):
            target_ref[high * 16 + low, rows, :] = tile


def second_kernel(vector, rate_ref, class_ref, x_ref, out_ref):
    chance = chances(rate_ref, vector)
    matrix = lane_matrix(chance)
    mix_low_devices(x_ref, out_ref, chance[19:23])

    @pl.loop(0, 16)
    def _(low):
        tiles = [[], []]
        for half in range(2):
            loaded = [out_ref[high * 16 + low, 8 * half : 8 * half + 8, :] for high in range(16)]
            tiles[half] = mix_bits(loaded, chance[23:27])
        for high in range(16):
            fitness = 0.5 + 0.25 * class_ref[high * 16 + low].astype(F32)
            scales = spread_fitness(jnp.concatenate([fitness, fitness], axis=1), 2)
            for half in range(2):
                tiles[half][high] = tiles[half][high] * scales[half]
        for half in range(2):
            tiles[half] = mix_lanes(tiles[half], matrix)
            tiles[half] = mix_sublanes(tiles[half], chance[7:10])
            tiles[half] = mix_bits(tiles[half], chance[23:27])
        for high in range(16):
            pair = mix_bits([tiles[0][high], tiles[1][high]], chance[10:11])
            for half in range(2):
                out_ref[high * 16 + low, 8 * half : 8 * half + 8, :] = pair[half]

    mix_low_devices(out_ref, out_ref, chance[19:23])


def third_kernel(vector, rate_ref, x_ref, out_ref):
    chance = chances(rate_ref, vector)
    mix_low_devices(x_ref, out_ref, chance[11:15])

    @pl.loop(0, 32)
    def _(at):
        low = at // 2
        rows = pl.ds(pl.multiple_of(8 * (at % 2), 8), 8)
        mixed = mix_bits([out_ref[high * 16 + low, rows, :] for high in range(16)], chance[15:19])
        for high, tile in enumerate(mixed):
            out_ref[high * 16 + low, rows, :] = tile


def last_kernel(vector, rate_ref, x_ref, other_ref, out_ref, held_ref):
    chance = chances(rate_ref, vector)
    mix_low_devices(x_ref, held_ref, chance[11:15])

    @pl.loop(0, 32)
    def _(at):
        low = at // 2
        half = at % 2
        rows = pl.ds(pl.multiple_of(8 * half, 8), 8)
        mixed = mix_bits([held_ref[high * 16 + low, rows, :] for high in range(16)], chance[15:19])
        for high, tile in enumerate(mixed):
            peer = high * 16 + low
            start = pl.multiple_of(peer * 32 + 16 * half, 16)
            out_ref[pl.ds(start + vector, 8, stride=2), :] = tile
            out_ref[pl.ds(start + 1 - vector, 8, stride=2), :] = other_ref[peer, rows, :]


SMEM = pl.BlockSpec(memory_space=pltpu.SMEM)
VMEM = pl.BlockSpec(memory_space=pltpu.VMEM)
PIECE = jax.ShapeDtypeStruct((DEVICES, PEER_ROWS, 128), F32)


def bind(kernel, vector):
    def bound(*refs):
        kernel(vector, *refs)

    return bound


def cost(flops, moved):
    return pl.CostEstimate(flops=flops, bytes_accessed=moved, transcendentals=0)


def first(vector, rate_index, classes, rows):
    return pl.pallas_call(
        bind(first_kernel, vector),
        out_shape=jax.ShapeDtypeStruct((LOCAL_ROWS, 128), F32),
        grid=(16,),
        in_specs=[
            SMEM,
            pl.BlockSpec((8, 128), lambda step: (step, 0)),
            pl.BlockSpec((512, 128), lambda step: (step, 0)),
        ],
        out_specs=pl.BlockSpec((LOCAL_ROWS, 128), lambda step: (0, 0)),
        cost_estimate=cost(1 << 29, 6 << 20),
        name="first",
    )(rate_index, classes, rows).reshape(PIECE.shape)


def second(vector, rate_index, classes, piece):
    return pl.pallas_call(
        bind(second_kernel, vector),
        out_shape=PIECE,
        in_specs=[SMEM, VMEM, VMEM],
        out_specs=VMEM,
        cost_estimate=cost(1 << 29, 4 << 20),
        name="second",
    )(rate_index, classes, piece)


def third(vector, rate_index, piece):
    return pl.pallas_call(
        bind(third_kernel, vector),
        out_shape=PIECE,
        in_specs=[SMEM, VMEM],
        out_specs=VMEM,
        cost_estimate=cost(1 << 29, 4 << 20),
        name="third",
    )(rate_index, piece)


def last(vector, rate_index, piece, other):
    return pl.pallas_call(
        bind(last_kernel, vector),
        out_shape=jax.ShapeDtypeStruct((2 * LOCAL_ROWS, 128), F32),
        in_specs=[SMEM, VMEM, VMEM],
        out_specs=VMEM,
        scratch_shapes=[pltpu.VMEM(PIECE.shape, F32)],
        cost_estimate=cost(1 << 29, 8 << 20),
        name="last",
    )(rate_index, piece, other)


def swap(piece):
    return lax.all_to_all(piece, AXES, split_axis=0, concat_axis=0, tiled=True)


def per_device(krylov, fitness_class, rate_index):
    rows = krylov.reshape(2, LOCAL_ROWS, 128).transpose(1, 0, 2).reshape(2 * LOCAL_ROWS, 128)
    classes = fitness_class.reshape(128, 128)
    moved_classes = swap(fitness_class.reshape(DEVICES, 1, 64))
    pieces = [swap(first(vector, rate_index, classes, rows)) for vector in range(2)]
    pieces = [swap(second(vector, rate_index, moved_classes, pieces[vector])) for vector in range(2)]
    done = third(0, rate_index, pieces[0])
    result = last(1, rate_index, pieces[1], done)
    return result.reshape(LOCAL_ROWS, 2, 128).transpose(1, 0, 2).reshape(2, LOCAL_ROWS * 128)


def solution(mesh):
    in_specs = (P(None, AXES), P(AXES), P())
    out_specs = P(None, AXES)
    return jax.shard_map(
        per_device, mesh=mesh, in_specs=in_specs, out_specs=out_specs, check_vma=False
    )
```

```python
import jax
import jax.numpy as jnp
import numpy as np
from jax import lax
from jax.experimental import pallas as pl
from jax.experimental.pallas import tpu as pltpu
from jax.sharding import PartitionSpec as P

AXES = ("wide", "narrow")
SITES = 27
RING = 8
PLANE = 32
REST = 16
PROFILE = [float(1.0 + 0.5 * np.cos(2.0 * site)) for site in range(SITES)]
RING_HERE = [16, 17, 18]
PLANE_HERE = [11, 12, 13, 14, 15]
RING_AWAY = [25, 26, 21]
PLANE_AWAY = [19, 20, 22, 23, 24]
F32 = jnp.float32
BF16 = jnp.bfloat16


def device_at(ring, plane):
    x, core, y = plane // 8, plane // 4 % 2, plane % 4
    return ((ring % 4 * 4 + x) * 2 + core) * 8 + ring // 4 * 4 + y


def ring_pairs(shift):
    return [
        (device_at(ring, plane), device_at((ring + shift) % RING, plane))
        for ring in range(RING)
        for plane in range(PLANE)
    ]


PLANE_GROUPS = [[device_at(ring, plane) for plane in range(PLANE)] for ring in range(RING)]


def chances(rate_ref, vector):
    level = 0.004 * (rate_ref[vector].astype(F32) + 1.0)
    return [level * PROFILE[site] for site in range(SITES)]


def pick(chance, sites):
    return [chance[site] for site in sites]


def mix_bits(tiles, chance_of_bit):
    tiles = list(tiles)
    for bit, chance in enumerate(chance_of_bit):
        step = 1 << bit
        for low in range(len(tiles)):
            if low & step:
                continue
            flow = chance * (tiles[low | step] - tiles[low])
            tiles[low] = tiles[low] + flow
            tiles[low | step] = tiles[low | step] - flow
    return tiles


def lane_matrix(chance):
    row = lax.broadcasted_iota(jnp.int32, (128, 128), 0)
    column = lax.broadcasted_iota(jnp.int32, (128, 128), 1)
    differ = row ^ column
    product = jnp.ones((128, 128), F32)
    for site in range(7):
        product = product * jnp.where((differ >> site) & 1 == 0, 1.0 - chance[site], chance[site])
    high = product.astype(BF16)
    low = (product - high.astype(F32)).astype(BF16)
    top = jnp.concatenate([high, low], axis=1)
    bottom = jnp.concatenate([high, jnp.zeros_like(low)], axis=1)
    return jnp.concatenate([top, bottom], axis=0)


def mix_lanes(tiles, matrix):
    rows = jnp.concatenate(tiles, axis=0)
    high = rows.astype(BF16)
    low = (rows - high.astype(F32)).astype(BF16)
    both = jnp.dot(jnp.concatenate([high, low], axis=1), matrix, preferred_element_type=F32)
    mixed = both[:, :128] + both[:, 128:]
    return [mixed[8 * at : 8 * at + 8] for at in range(len(tiles))]


def mix_sublanes(tiles, chance):
    sub = lax.broadcasted_iota(jnp.int32, (8, 128), 0)
    mixed = []
    for tile in tiles:
        for bit in range(3):
            step = 1 << bit
            if step == 4:
                partner = pltpu.roll(tile, 4, 0)
            else:
                partner = jnp.where(
                    sub & step == 0, pltpu.roll(tile, 8 - step, 0), pltpu.roll(tile, step, 0)
                )
            tile = tile + chance[bit] * (partner - tile)
        mixed.append(tile)
    return mixed


def mix_rest(tiles, chance, matrix):
    tiles = mix_sublanes(mix_lanes(tiles, matrix), chance[7:10])
    paired = []
    for at in range(0, len(tiles), 2):
        paired += mix_bits(tiles[at : at + 2], chance[10:11])
    return paired


def spread(row, pattern):
    sub = lax.broadcasted_iota(jnp.int32, (8, 128), 0)
    lane = lax.broadcasted_iota(jnp.int32, (8, 128), 1)
    index = 4 * (8 * pattern + sub) + (lane >> 5)
    return jnp.take_along_axis(
        jnp.broadcast_to(row, (8, 128)), index, axis=1, mode="promise_in_bounds"
    )


def half_rows(half):
    return pl.ds(pl.multiple_of(8 * half, 8), 8)


def mix_ring(held, chance):
    @pl.loop(0, 2 * PLANE, unroll=4)
    def _(at):
        plane, rows = at // 2, half_rows(at % 2)
        mixed = mix_bits([held[ring, plane, rows, :] for ring in range(RING)], chance)
        for ring in range(RING):
            held[ring, plane, rows, :] = mixed[ring]


def mix_plane(held, ring, chance):
    for half in range(2):
        rows = pl.ds(8 * half, 8)
        mixed = mix_bits([held[ring, plane, rows, :] for plane in range(PLANE)], chance)
        for plane in range(PLANE):
            held[ring, plane, rows, :] = mixed[plane]


def my_ring():
    return lax.axis_index("narrow") // 4 * 4 + lax.axis_index("wide") // 8


def ring_slot(shift):
    return lax.rem(my_ring() + shift + RING, RING)


def from_ring(refs, held, sems):
    def copies():
        return [
            pltpu.make_async_copy(ref, held.at[ring_slot(-shift)], sems.at[shift])
            for shift, ref in enumerate(refs)
        ]

    return copies


def to_ring(held, refs, sems):
    def copies():
        return [
            pltpu.make_async_copy(held.at[ring_slot(shift)], ref, sems.at[shift])
            for shift, ref in enumerate(refs)
        ]

    return copies


def plane_copy(ref, held, ring, sems, outward=False):
    rows = pl.ds(pl.multiple_of(REST * ring, REST), REST)
    here, there = held.at[ring], ref.at[:, rows, :]
    if outward:
        return pltpu.make_async_copy(here, there, sems.at[ring])
    return pltpu.make_async_copy(there, here, sems.at[ring])


def start_all(copies):
    for copy in copies:
        copy.start()


def wait_all(copies):
    for copy in copies:
        copy.wait()


def begin_ring(rate_ref, class_ref, x_ref, *refs):
    outs, (x_held, class_held, held, in_sems, out_sems, class_sem) = refs[:RING], refs[RING:]
    chance = chances(rate_ref, 0)

    def load(part):
        rows = pl.ds(pl.multiple_of(128 * part, 128), 128)
        return pltpu.make_async_copy(
            x_ref.at[:, rows, :], x_held.at[:, rows, :], in_sems.at[part]
        )

    classes = pltpu.make_async_copy(class_ref, class_held, class_sem)
    classes.start()
    for part in range(RING):
        load(part).start()
    classes.wait()
    for ring in range(RING):
        held[ring, PLANE] = 0.5 + 0.25 * class_held[REST * ring : REST * ring + REST].astype(F32)

    @pl.loop(0, RING)
    def _(part):
        load(part).wait()
        for at in range(8):
            plane, rows = 4 * part + at // 2, pl.ds(8 * (at % 2), 8)
            tiles = []
            for ring in range(RING):
                scale = spread(held[ring, PLANE, pl.ds(2 * part + at // 4, 1), :], at % 4)
                start = pl.multiple_of(128 * part + 16 * at, 16)
                tiles.append(x_held[ring, pl.ds(start, 8, stride=2), :] * scale)
            for ring, tile in enumerate(mix_bits(tiles, pick(chance, RING_HERE))):
                held[ring, plane, rows, :] = tile

    copies = to_ring(held, outs, out_sems)()
    start_all(copies)
    wait_all(copies)


def begin_plane(rate_ref, class_ref, x_ref, out_ref, x_held, class_held, held, in_sems, out_sems, class_sem):
    chance = chances(rate_ref, 1)

    def load(ring):
        return pltpu.make_async_copy(x_ref.at[ring], x_held.at[ring], in_sems.at[ring])

    classes = pltpu.make_async_copy(class_ref, class_held, class_sem)
    classes.start()
    for ring in range(RING):
        load(ring).start()
    classes.wait()

    @pl.loop(0, RING)
    def _(ring):
        load(ring).wait()
        first_row = pl.multiple_of(REST * ring, REST)
        fitness = 0.5 + 0.25 * class_held[pl.ds(first_row, REST), :].astype(F32)
        for half in range(2):
            tiles = []
            for plane in range(PLANE):
                scale = spread(fitness[plane // 2 : plane // 2 + 1], plane % 2 * 2 + half)
                tiles.append(x_held[ring, pl.ds(32 * plane + 16 * half + 1, 8, stride=2), :] * scale)
            for plane, tile in enumerate(mix_bits(tiles, pick(chance, PLANE_HERE))):
                held[ring, plane, pl.ds(8 * half, 8), :] = tile
        plane_copy(out_ref, held, ring, out_sems, outward=True).start()

    wait_all([plane_copy(out_ref, held, ring, out_sems, outward=True) for ring in range(RING)])


def ring_to_plane_first(rate_ref, *refs):
    parts, out_ref, (held, rows_held, in_sems, out_sems, row_sem) = refs[:RING], refs[RING], refs[RING + 1 :]
    chance = chances(rate_ref, 0)
    copies = from_ring(parts, held, in_sems)()
    start_all(copies)
    wait_all(copies)
    for ring in range(RING):
        straight = held[ring, PLANE]
        turned = pltpu.roll(straight, 64, 1)
        for pair in range(REST):
            rows_held[2 * pair, ring : ring + 1, :] = straight[pair : pair + 1]
            rows_held[2 * pair + 1, ring : ring + 1, :] = turned[pair : pair + 1]
    rows_copy = pltpu.make_async_copy(rows_held, out_ref.at[:, pl.ds(RING * REST, RING), :], row_sem)
    rows_copy.start()
    mix_ring(held, pick(chance, RING_AWAY))

    def send(ring):
        return plane_copy(out_ref, held.at[:, pl.ds(0, PLANE)], ring, out_sems, outward=True)

    @pl.loop(0, RING)
    def _(ring):
        mix_plane(held, ring, pick(chance, PLANE_HERE))
        send(ring).start()

    wait_all([send(ring) for ring in range(RING)])
    rows_copy.wait()


def apply_middle(held, rows_held, ring, chance, matrix):
    @pl.loop(0, 4)
    def _(eighth):
        places = [(8 * eighth + at // 2, pl.ds(8 * (at % 2), 8)) for at in range(16)]
        tiles = [held[ring, plane, rows, :] for plane, rows in places]
        tiles = mix_rest(tiles, chance, matrix)
        for at, (plane, _) in enumerate(places):
            tiles[at] = tiles[at] * spread(rows_held[plane, pl.ds(ring, 1), :], at % 2)
        tiles = mix_rest(tiles, chance, matrix)
        for (plane, rows), tile in zip(places, tiles):
            held[ring, plane, rows, :] = tile


def middle_ring(rate_ref, x_ref, *refs):
    outs, (held, rows_held, in_sems, out_sems, row_sem) = refs[:RING], refs[RING:]
    chance = chances(rate_ref, 0)
    rows_copy = pltpu.make_async_copy(x_ref.at[:, pl.ds(RING * REST, RING), :], rows_held, row_sem)
    rows_copy.start()
    start_all([plane_copy(x_ref, held, ring, in_sems) for ring in range(RING)])
    matrix = lane_matrix(chance)
    rows_copy.wait()

    @pl.loop(0, RING)
    def _(ring):
        plane_copy(x_ref, held, ring, in_sems).wait()
        mix_plane(held, ring, pick(chance, PLANE_AWAY))
        apply_middle(held, rows_held, ring, chance, matrix)
        mix_plane(held, ring, pick(chance, PLANE_AWAY))

    mix_ring(held, pick(chance, RING_AWAY))
    copies = to_ring(held, outs, out_sems)()
    start_all(copies)
    wait_all(copies)


def ring_to_plane(rate_ref, *refs):
    parts, out_ref, (held, in_sems, out_sems) = refs[:RING], refs[RING], refs[RING + 1 :]
    chance = chances(rate_ref, 0)
    copies = from_ring(parts, held, in_sems)()
    start_all(copies)
    wait_all(copies)
    mix_ring(held, pick(chance, RING_HERE))
    copies = [plane_copy(out_ref, held, ring, out_sems, outward=True) for ring in range(RING)]
    start_all(copies)
    wait_all(copies)


def end_plane(rate_ref, x_ref, out_ref, held, in_sems, out_sems):
    chance = chances(rate_ref, 0)
    start_all([plane_copy(x_ref, held, ring, in_sems) for ring in range(RING)])

    def send(ring):
        return pltpu.make_async_copy(held.at[ring], out_ref.at[ring], out_sems.at[ring])

    @pl.loop(0, RING)
    def _(ring):
        plane_copy(x_ref, held, ring, in_sems).wait()
        mix_plane(held, ring, pick(chance, PLANE_HERE))
        send(ring).start()

    wait_all([send(ring) for ring in range(RING)])


def plane_to_ring(plane_sites, ring_sites):
    def kernel(rate_ref, x_ref, *refs):
        outs, (held, in_sems, out_sems) = refs[:RING], refs[RING:]
        chance = chances(rate_ref, 1)
        start_all([plane_copy(x_ref, held, ring, in_sems) for ring in range(RING)])

        @pl.loop(0, RING)
        def _(ring):
            plane_copy(x_ref, held, ring, in_sems).wait()
            mix_plane(held, ring, pick(chance, plane_sites))

        if ring_sites:
            mix_ring(held, pick(chance, ring_sites))
        copies = to_ring(held, outs, out_sems)()
        start_all(copies)
        wait_all(copies)

    return kernel


def middle_plane(rate_ref, fitness_ref, *refs):
    parts, out_ref, (held, rows_held, in_sems, out_sems, row_sem) = refs[:RING], refs[RING], refs[RING + 1 :]
    chance = chances(rate_ref, 1)
    rows_copy = pltpu.make_async_copy(fitness_ref.at[:, pl.ds(RING * REST, RING), :], rows_held, row_sem)
    rows_copy.start()
    copies = from_ring(parts, held, in_sems)()
    start_all(copies)
    matrix = lane_matrix(chance)
    rows_copy.wait()
    wait_all(copies)
    mix_ring(held, pick(chance, RING_AWAY))

    @pl.loop(0, RING)
    def _(ring):
        apply_middle(held, rows_held, ring, chance, matrix)
        mix_plane(held, ring, pick(chance, PLANE_AWAY))

    mix_ring(held, pick(chance, RING_AWAY))
    copies = [plane_copy(out_ref, held, ring, out_sems, outward=True) for ring in range(RING)]
    start_all(copies)
    wait_all(copies)


def end_ring(rate_ref, other_ref, *refs):
    parts, out_ref, (held, other_held, out_held, in_sems, other_sems, out_sems) = refs[:RING], refs[RING], refs[RING + 1 :]
    chance = chances(rate_ref, 1)
    other_copies = [
        pltpu.make_async_copy(other_ref.at[ring], other_held.at[ring], other_sems.at[ring])
        for ring in range(RING)
    ]
    copies = from_ring(parts, held, in_sems)()
    start_all(copies + other_copies)
    wait_all(copies + other_copies)

    def send(part):
        rows = pl.ds(pl.multiple_of(128 * part, 128), 128)
        return pltpu.make_async_copy(
            out_held.at[:, rows, :], out_ref.at[:, rows, :], out_sems.at[part]
        )

    @pl.loop(0, RING)
    def _(part):
        for at in range(8):
            plane, rows = 4 * part + at // 2, pl.ds(8 * (at % 2), 8)
            start = pl.multiple_of(128 * part + 16 * at, 16)
            tiles = [held[ring, plane, rows, :] for ring in range(RING)]
            for ring, tile in enumerate(mix_bits(tiles, pick(chance, RING_HERE))):
                out_held[ring, pl.ds(start, 8, stride=2), :] = other_held[ring, plane, rows, :]
                out_held[ring, pl.ds(start + 1, 8, stride=2), :] = tile
        send(part).start()

    wait_all([send(part) for part in range(RING)])


SMEM = pl.BlockSpec(memory_space=pltpu.SMEM)
ANY = pl.BlockSpec(memory_space=pl.ANY)
HELD = pltpu.VMEM((RING, PLANE, REST, 128), F32)
HELD_MORE = pltpu.VMEM((RING, PLANE + 1, REST, 128), F32)
WHOLE = pltpu.VMEM((RING, 1024, 128), F32)
CLASSES = pltpu.VMEM((128, 128), jnp.int32)
ROWS = pltpu.VMEM((PLANE, RING, 128), F32)
EIGHT = pltpu.SemaphoreType.DMA((RING,))
ONE = pltpu.SemaphoreType.DMA
SENT_RING = [jax.ShapeDtypeStruct((PLANE, REST, 128), F32)] * RING
SENT_RING_MORE = [jax.ShapeDtypeStruct((PLANE + 1, REST, 128), F32)] * RING
SENT_PLANE = jax.ShapeDtypeStruct((PLANE, RING * REST, 128), F32)
SENT_PLANE_MORE = jax.ShapeDtypeStruct((PLANE, RING * REST + RING, 128), F32)


def call(kernel, name, outs, scratch, rate_index, *operands):
    many = isinstance(outs, list)
    with jax.named_scope(name):
        return pl.pallas_call(
            kernel,
            out_shape=outs,
            in_specs=[SMEM] + [ANY] * len(operands),
            out_specs=[ANY] * len(outs) if many else ANY,
            scratch_shapes=scratch,
            cost_estimate=pl.CostEstimate(
                flops=1 << 28, bytes_accessed=8 << 20, transcendentals=0
            ),
            name=name,
        )(rate_index, *operands)


def round_ring(parts, name):
    with jax.named_scope(name):
        return [parts[0]] + [
            lax.ppermute(part, AXES, ring_pairs(shift))
            for shift, part in enumerate(parts)
            if shift
        ]


def in_plane(piece, name):
    with jax.named_scope(name):
        return lax.all_to_all(
            piece, AXES, split_axis=0, concat_axis=0, tiled=True, axis_index_groups=PLANE_GROUPS
        )


def per_device(krylov, fitness_class, rate_index):
    rows = krylov.reshape(2, 4096, 128).transpose(1, 0, 2).reshape(RING, 1024, 128)
    classes = fitness_class.reshape(128, 128)
    rate = rate_index
    begin = [WHOLE, CLASSES]
    ends = [EIGHT, EIGHT]

    a = call(begin_ring, "a1", SENT_RING_MORE, begin + [HELD_MORE] + ends + [ONE], rate, classes, rows)
    a = round_ring(a, "az1")
    b = call(begin_plane, "b1", SENT_PLANE, begin + [HELD] + ends + [ONE], rate, classes, rows)
    b = in_plane(b, "bx1")
    b = call(plane_to_ring(PLANE_AWAY, RING_HERE), "b2", SENT_RING, [HELD] + ends, rate, b)
    b = round_ring(b, "bz1")
    a = call(ring_to_plane_first, "a2", SENT_PLANE_MORE, [HELD_MORE, ROWS] + ends + [ONE], rate, *a)
    a = in_plane(a, "ax1")
    fitness = a
    a = call(middle_ring, "a3", SENT_RING, [HELD, ROWS] + ends + [ONE], rate, a)
    a = round_ring(a, "az2")
    b = call(middle_plane, "b3", SENT_PLANE, [HELD, ROWS] + ends + [ONE], rate, fitness, *b)
    b = in_plane(b, "bx2")
    b = call(plane_to_ring(PLANE_HERE, []), "b4", SENT_RING, [HELD] + ends, rate, b)
    b = round_ring(b, "bz2")
    a = call(ring_to_plane, "a4", SENT_PLANE, [HELD] + ends, rate, *a)
    a = in_plane(a, "ax2")
    done = jax.ShapeDtypeStruct((RING, PLANE, REST, 128), F32)
    a = call(end_plane, "a5", done, [HELD] + ends, rate, a)
    whole = jax.ShapeDtypeStruct((RING, 1024, 128), F32)
    result = call(end_ring, "b5", whole, [HELD, HELD, WHOLE, EIGHT] + ends, rate, a, *b)
    return result.reshape(4096, 2, 128).transpose(1, 0, 2).reshape(2, 4096 * 128)


def solution(mesh):
    in_specs = (P(None, AXES), P(AXES), P())
    out_specs = P(None, AXES)
    return jax.shard_map(
        per_device, mesh=mesh, in_specs=in_specs, out_specs=out_specs, check_vma=False
    )
```

```python
import jax
import jax.numpy as jnp
import numpy as np
from jax import lax
from jax.experimental import pallas as pl
from jax.experimental.pallas import tpu as pltpu
from jax.sharding import PartitionSpec as P


AXES = ("wide", "narrow")
SITES = 27
RING = 8
PLANE = 32
REST = 16
PROFILE = [float(1.0 + 0.5 * np.cos(2.0 * site)) for site in range(SITES)]
RING_HERE = [16, 17, 18]
PLANE_HERE = [11, 12, 13, 14, 15]
RING_AWAY = [25, 26, 21]
PLANE_AWAY = [19, 20, 22, 23, 24]
F32 = jnp.float32
BF16 = jnp.bfloat16


def device_at(ring, plane):
    x, core, y = plane // 8, plane // 4 % 2, plane % 4
    return ((ring % 4 * 4 + x) * 2 + core) * 8 + ring // 4 * 4 + y


def ring_pairs(shift):
    return [
        (device_at(ring, plane), device_at((ring + shift) % RING, plane))
        for ring in range(RING)
        for plane in range(PLANE)
    ]


PLANE_GROUPS = [[device_at(ring, plane) for plane in range(PLANE)] for ring in range(RING)]


def chances(rate_ref, vector):
    level = 0.004 * (rate_ref[vector].astype(F32) + 1.0)
    return [level * PROFILE[site] for site in range(SITES)]


def pick(chance, sites):
    return [chance[site] for site in sites]


def mix_bits(tiles, chance_of_bit):
    tiles = list(tiles)
    for bit, chance in enumerate(chance_of_bit):
        step = 1 << bit
        for low in range(len(tiles)):
            if low & step:
                continue
            flow = chance * (tiles[low | step] - tiles[low])
            tiles[low] = tiles[low] + flow
            tiles[low | step] = tiles[low | step] - flow
    return tiles


def lane_matrix(chance):
    row = lax.broadcasted_iota(jnp.int32, (128, 128), 0)
    column = lax.broadcasted_iota(jnp.int32, (128, 128), 1)
    differ = row ^ column
    product = jnp.ones((128, 128), F32)
    for site in range(7):
        product = product * jnp.where((differ >> site) & 1 == 0, 1.0 - chance[site], chance[site])
    high = product.astype(BF16)
    low = (product - high.astype(F32)).astype(BF16)
    top = jnp.concatenate([high, low], axis=1)
    bottom = jnp.concatenate([high, jnp.zeros_like(low)], axis=1)
    return jnp.concatenate([top, bottom], axis=0)


def mix_lanes(tiles, matrix):
    rows = jnp.concatenate(tiles, axis=0)
    high = rows.astype(BF16)
    low = (rows - high.astype(F32)).astype(BF16)
    both = jnp.dot(jnp.concatenate([high, low], axis=1), matrix, preferred_element_type=F32)
    mixed = both[:, :128] + both[:, 128:]
    return [mixed[8 * at : 8 * at + 8] for at in range(len(tiles))]


def mix_sublanes(tiles, chance):
    sub = lax.broadcasted_iota(jnp.int32, (8, 128), 0)
    mixed = []
    for tile in tiles:
        for bit in range(3):
            step = 1 << bit
            if step == 4:
                partner = pltpu.roll(tile, 4, 0)
            else:
                partner = jnp.where(
                    sub & step == 0, pltpu.roll(tile, 8 - step, 0), pltpu.roll(tile, step, 0)
                )
            tile = tile + chance[bit] * (partner - tile)
        mixed.append(tile)
    return mixed


def mix_rest(tiles, chance, matrix):
    tiles = mix_sublanes(mix_lanes(tiles, matrix), chance[7:10])
    paired = []
    for at in range(0, len(tiles), 2):
        paired += mix_bits(tiles[at : at + 2], chance[10:11])
    return paired


def spread(row, pattern):
    sub = lax.broadcasted_iota(jnp.int32, (8, 128), 0)
    lane = lax.broadcasted_iota(jnp.int32, (8, 128), 1)
    index = 4 * (8 * pattern + sub) + (lane >> 5)
    return jnp.take_along_axis(
        jnp.broadcast_to(row, (8, 128)), index, axis=1, mode="promise_in_bounds"
    )


def half_rows(half):
    return pl.ds(pl.multiple_of(8 * half, 8), 8)


def mix_ring(held, chance):
    @pl.loop(0, 2 * PLANE, unroll=4)
    def _(at):
        plane, rows = at // 2, half_rows(at % 2)
        mixed = mix_bits([held[ring, plane, rows, :] for ring in range(RING)], chance)
        for ring in range(RING):
            held[ring, plane, rows, :] = mixed[ring]


def mix_plane(held, ring, chance):
    for half in range(2):
        rows = pl.ds(8 * half, 8)
        mixed = mix_bits([held[ring, plane, rows, :] for plane in range(PLANE)], chance)
        for plane in range(PLANE):
            held[ring, plane, rows, :] = mixed[plane]


def my_ring():
    return lax.axis_index("narrow") // 4 * 4 + lax.axis_index("wide") // 8


def ring_slot(shift):
    return lax.rem(my_ring() + shift + RING, RING)


def from_ring(refs, held, sems):
    def copies():
        return [
            pltpu.make_async_copy(ref, held.at[ring_slot(-shift)], sems.at[shift])
            for shift, ref in enumerate(refs)
        ]

    return copies


def to_ring(held, refs, sems):
    def copies():
        return [
            pltpu.make_async_copy(held.at[ring_slot(shift)], ref, sems.at[shift])
            for shift, ref in enumerate(refs)
        ]

    return copies


def plane_copy(ref, held, ring, sems, outward=False):
    rows = pl.ds(pl.multiple_of(REST * ring, REST), REST)
    here, there = held.at[ring], ref.at[:, rows, :]
    if outward:
        return pltpu.make_async_copy(here, there, sems.at[ring])
    return pltpu.make_async_copy(there, here, sems.at[ring])


def start_all(copies):
    for copy in copies:
        copy.start()


def wait_all(copies):
    for copy in copies:
        copy.wait()


def begin_ring(rate_ref, class_ref, x_ref, *refs):
    outs, (x_held, class_held, held, in_sems, out_sems, class_sem) = refs[:RING], refs[RING:]
    chance = chances(rate_ref, 0)

    def load(part):
        rows = pl.ds(pl.multiple_of(128 * part, 128), 128)
        return pltpu.make_async_copy(
            x_ref.at[:, rows, :], x_held.at[:, rows, :], in_sems.at[part]
        )

    classes = pltpu.make_async_copy(class_ref, class_held, class_sem)
    classes.start()
    for part in range(RING):
        load(part).start()
    classes.wait()
    for ring in range(RING):
        held[ring, PLANE] = 0.5 + 0.25 * class_held[REST * ring : REST * ring + REST].astype(F32)

    @pl.loop(0, RING)
    def _(part):
        load(part).wait()
        for at in range(8):
            plane, rows = 4 * part + at // 2, pl.ds(8 * (at % 2), 8)
            tiles = []
            for ring in range(RING):
                scale = spread(held[ring, PLANE, pl.ds(2 * part + at // 4, 1), :], at % 4)
                start = pl.multiple_of(128 * part + 16 * at, 16)
                tiles.append(x_held[ring, pl.ds(start, 8, stride=2), :] * scale)
            for ring, tile in enumerate(mix_bits(tiles, pick(chance, RING_HERE))):
                held[ring, plane, rows, :] = tile

    copies = to_ring(held, outs, out_sems)()
    start_all(copies)
    wait_all(copies)


def begin_plane(rate_ref, class_ref, x_ref, out_ref, x_held, class_held, held, in_sems, out_sems, class_sem):
    chance = chances(rate_ref, 1)

    def load(ring):
        return pltpu.make_async_copy(x_ref.at[ring], x_held.at[ring], in_sems.at[ring])

    classes = pltpu.make_async_copy(class_ref, class_held, class_sem)
    classes.start()
    for ring in range(RING):
        load(ring).start()
    classes.wait()

    @pl.loop(0, RING)
    def _(ring):
        load(ring).wait()
        first_row = pl.multiple_of(REST * ring, REST)
        fitness = 0.5 + 0.25 * class_held[pl.ds(first_row, REST), :].astype(F32)
        for half in range(2):
            tiles = []
            for plane in range(PLANE):
                scale = spread(fitness[plane // 2 : plane // 2 + 1], plane % 2 * 2 + half)
                tiles.append(x_held[ring, pl.ds(32 * plane + 16 * half + 1, 8, stride=2), :] * scale)
            for plane, tile in enumerate(mix_bits(tiles, pick(chance, PLANE_HERE))):
                held[ring, plane, pl.ds(8 * half, 8), :] = tile
        plane_copy(out_ref, held, ring, out_sems, outward=True).start()

    wait_all([plane_copy(out_ref, held, ring, out_sems, outward=True) for ring in range(RING)])


def ring_to_plane_first(rate_ref, *refs):
    parts, out_ref, (held, rows_held, in_sems, out_sems, row_sem) = refs[:RING], refs[RING], refs[RING + 1 :]
    chance = chances(rate_ref, 0)
    copies = from_ring(parts, held, in_sems)()
    start_all(copies)
    wait_all(copies)
    for ring in range(RING):
        straight = held[ring, PLANE]
        turned = pltpu.roll(straight, 64, 1)
        for pair in range(REST):
            rows_held[2 * pair, ring : ring + 1, :] = straight[pair : pair + 1]
            rows_held[2 * pair + 1, ring : ring + 1, :] = turned[pair : pair + 1]
    rows_copy = pltpu.make_async_copy(rows_held, out_ref.at[:, pl.ds(RING * REST, RING), :], row_sem)
    rows_copy.start()
    mix_ring(held, pick(chance, RING_AWAY))

    def send(ring):
        return plane_copy(out_ref, held.at[:, pl.ds(0, PLANE)], ring, out_sems, outward=True)

    @pl.loop(0, RING)
    def _(ring):
        mix_plane(held, ring, pick(chance, PLANE_HERE))
        send(ring).start()

    wait_all([send(ring) for ring in range(RING)])
    rows_copy.wait()


def apply_middle(held, rows_held, ring, chance, matrix):
    @pl.loop(0, 4)
    def _(eighth):
        places = [(8 * eighth + at // 2, pl.ds(8 * (at % 2), 8)) for at in range(16)]
        tiles = [held[ring, plane, rows, :] for plane, rows in places]
        tiles = mix_rest(tiles, chance, matrix)
        for at, (plane, _) in enumerate(places):
            tiles[at] = tiles[at] * spread(rows_held[plane, pl.ds(ring, 1), :], at % 2)
        tiles = mix_rest(tiles, chance, matrix)
        for (plane, rows), tile in zip(places, tiles):
            held[ring, plane, rows, :] = tile


def middle_ring(rate_ref, x_ref, *refs):
    outs, (held, rows_held, in_sems, out_sems, row_sem) = refs[:RING], refs[RING:]
    chance = chances(rate_ref, 0)
    rows_copy = pltpu.make_async_copy(x_ref.at[:, pl.ds(RING * REST, RING), :], rows_held, row_sem)
    rows_copy.start()
    start_all([plane_copy(x_ref, held, ring, in_sems) for ring in range(RING)])
    matrix = lane_matrix(chance)
    rows_copy.wait()

    @pl.loop(0, RING)
    def _(ring):
        plane_copy(x_ref, held, ring, in_sems).wait()
        mix_plane(held, ring, pick(chance, PLANE_AWAY))
        apply_middle(held, rows_held, ring, chance, matrix)
        mix_plane(held, ring, pick(chance, PLANE_AWAY))

    mix_ring(held, pick(chance, RING_AWAY))
    copies = to_ring(held, outs, out_sems)()
    start_all(copies)
    wait_all(copies)


def ring_to_plane(rate_ref, *refs):
    parts, out_ref, (held, in_sems, out_sems) = refs[:RING], refs[RING], refs[RING + 1 :]
    chance = chances(rate_ref, 0)
    copies = from_ring(parts, held, in_sems)()
    start_all(copies)
    wait_all(copies)
    mix_ring(held, pick(chance, RING_HERE))
    copies = [plane_copy(out_ref, held, ring, out_sems, outward=True) for ring in range(RING)]
    start_all(copies)
    wait_all(copies)


def end_plane(rate_ref, x_ref, out_ref, held, in_sems, out_sems):
    chance = chances(rate_ref, 0)
    start_all([plane_copy(x_ref, held, ring, in_sems) for ring in range(RING)])

    def send(ring):
        return pltpu.make_async_copy(held.at[ring], out_ref.at[ring], out_sems.at[ring])

    @pl.loop(0, RING)
    def _(ring):
        plane_copy(x_ref, held, ring, in_sems).wait()
        mix_plane(held, ring, pick(chance, PLANE_HERE))
        send(ring).start()

    wait_all([send(ring) for ring in range(RING)])


def plane_to_ring(plane_sites, ring_sites):
    def kernel(rate_ref, x_ref, *refs):
        outs, (held, in_sems, out_sems) = refs[:RING], refs[RING:]
        chance = chances(rate_ref, 1)
        start_all([plane_copy(x_ref, held, ring, in_sems) for ring in range(RING)])

        @pl.loop(0, RING)
        def _(ring):
            plane_copy(x_ref, held, ring, in_sems).wait()
            mix_plane(held, ring, pick(chance, plane_sites))

        if ring_sites:
            mix_ring(held, pick(chance, ring_sites))
        copies = to_ring(held, outs, out_sems)()
        start_all(copies)
        wait_all(copies)

    return kernel


def middle_plane(rate_ref, fitness_ref, *refs):
    parts, out_ref, (held, rows_held, in_sems, out_sems, row_sem) = refs[:RING], refs[RING], refs[RING + 1 :]
    chance = chances(rate_ref, 1)
    rows_copy = pltpu.make_async_copy(fitness_ref.at[:, pl.ds(RING * REST, RING), :], rows_held, row_sem)
    rows_copy.start()
    copies = from_ring(parts, held, in_sems)()
    start_all(copies)
    matrix = lane_matrix(chance)
    rows_copy.wait()
    wait_all(copies)
    mix_ring(held, pick(chance, RING_AWAY))

    @pl.loop(0, RING)
    def _(ring):
        apply_middle(held, rows_held, ring, chance, matrix)
        mix_plane(held, ring, pick(chance, PLANE_AWAY))

    mix_ring(held, pick(chance, RING_AWAY))
    copies = [plane_copy(out_ref, held, ring, out_sems, outward=True) for ring in range(RING)]
    start_all(copies)
    wait_all(copies)


def end_ring(rate_ref, other_ref, *refs):
    parts, out_ref, (held, other_held, out_held, in_sems, other_sems, out_sems) = refs[:RING], refs[RING], refs[RING + 1 :]
    chance = chances(rate_ref, 1)
    other_copies = [
        pltpu.make_async_copy(other_ref.at[ring], other_held.at[ring], other_sems.at[ring])
        for ring in range(RING)
    ]
    copies = from_ring(parts, held, in_sems)()
    start_all(copies + other_copies)
    wait_all(copies + other_copies)

    def send(part):
        rows = pl.ds(pl.multiple_of(128 * part, 128), 128)
        return pltpu.make_async_copy(
            out_held.at[:, rows, :], out_ref.at[:, rows, :], out_sems.at[part]
        )

    @pl.loop(0, RING)
    def _(part):
        for at in range(8):
            plane, rows = 4 * part + at // 2, pl.ds(8 * (at % 2), 8)
            start = pl.multiple_of(128 * part + 16 * at, 16)
            tiles = [held[ring, plane, rows, :] for ring in range(RING)]
            for ring, tile in enumerate(mix_bits(tiles, pick(chance, RING_HERE))):
                out_held[ring, pl.ds(start, 8, stride=2), :] = other_held[ring, plane, rows, :]
                out_held[ring, pl.ds(start + 1, 8, stride=2), :] = tile
        send(part).start()

    wait_all([send(part) for part in range(RING)])


SMEM = pl.BlockSpec(memory_space=pltpu.SMEM)
ANY = pl.BlockSpec(memory_space=pl.ANY)
HELD = pltpu.VMEM((RING, PLANE, REST, 128), F32)
HELD_MORE = pltpu.VMEM((RING, PLANE + 1, REST, 128), F32)
WHOLE = pltpu.VMEM((RING, 1024, 128), F32)
CLASSES = pltpu.VMEM((128, 128), jnp.int32)
ROWS = pltpu.VMEM((PLANE, RING, 128), F32)
EIGHT = pltpu.SemaphoreType.DMA((RING,))
ONE = pltpu.SemaphoreType.DMA
SENT_RING = [jax.ShapeDtypeStruct((PLANE, REST, 128), F32)] * RING
SENT_RING_MORE = [jax.ShapeDtypeStruct((PLANE + 1, REST, 128), F32)] * RING
SENT_PLANE = jax.ShapeDtypeStruct((PLANE, RING * REST, 128), F32)
SENT_PLANE_MORE = jax.ShapeDtypeStruct((PLANE, RING * REST + RING, 128), F32)


def call(kernel, name, outs, scratch, rate_index, *operands):
    many = isinstance(outs, list)
    return pl.pallas_call(
        kernel,
        out_shape=outs,
        in_specs=[SMEM] + [ANY] * len(operands),
        out_specs=[ANY] * len(outs) if many else ANY,
        scratch_shapes=scratch,
        cost_estimate=pl.CostEstimate(
            flops=1 << 28, bytes_accessed=8 << 20, transcendentals=0
        ),
        compiler_params=pltpu.CompilerParams(vmem_limit_bytes=(56 if name in ("a1", "b1") else 16) << 20),
    )(rate_index, *operands)


def round_ring(parts):
    return [parts[0]] + [
        lax.ppermute(part, AXES, ring_pairs(shift))
        for shift, part in enumerate(parts)
        if shift
    ]


def in_plane(piece):
    return lax.all_to_all(
        piece, AXES, split_axis=0, concat_axis=0, tiled=True, axis_index_groups=PLANE_GROUPS
    )


def per_device(krylov, fitness_class, rate_index):
    rows = krylov.reshape(2, 4096, 128).transpose(1, 0, 2).reshape(RING, 1024, 128)
    classes = fitness_class.reshape(128, 128)
    rate = rate_index
    begin = [WHOLE, CLASSES]
    ends = [EIGHT, EIGHT]

    a = call(begin_ring, "a1", SENT_RING_MORE, begin + [HELD_MORE] + ends + [ONE], rate, classes, rows)
    a = round_ring(a)
    b = call(begin_plane, "b1", SENT_PLANE, begin + [HELD] + ends + [ONE], rate, classes, rows)
    b = in_plane(b)
    b = call(plane_to_ring(PLANE_AWAY, RING_HERE), "b2", SENT_RING, [HELD] + ends, rate, b)
    b = round_ring(b)
    a = call(ring_to_plane_first, "a2", SENT_PLANE_MORE, [HELD_MORE, ROWS] + ends + [ONE], rate, *a)
    a = in_plane(a)
    fitness = a
    a = call(middle_ring, "a3", SENT_RING, [HELD, ROWS] + ends + [ONE], rate, a)
    a = round_ring(a)
    b = call(middle_plane, "b3", SENT_PLANE, [HELD, ROWS] + ends + [ONE], rate, fitness, *b)
    b = in_plane(b)
    b = call(plane_to_ring(PLANE_HERE, []), "b4", SENT_RING, [HELD] + ends, rate, b)
    b = round_ring(b)
    a = call(ring_to_plane, "a4", SENT_PLANE, [HELD] + ends, rate, *a)
    a = in_plane(a)
    done = jax.ShapeDtypeStruct((RING, PLANE, REST, 128), F32)
    a = call(end_plane, "a5", done, [HELD] + ends, rate, a)
    whole = jax.ShapeDtypeStruct((RING, 1024, 128), F32)
    result = call(end_ring, "b5", whole, [HELD, HELD, WHOLE, EIGHT] + ends, rate, a, *b)
    return result.reshape(4096, 2, 128).transpose(1, 0, 2).reshape(2, 4096 * 128)


def solution(mesh):
    in_specs = (P(None, AXES), P(AXES), P())
    out_specs = P(None, AXES)
    return jax.shard_map(per_device, mesh=mesh, in_specs=in_specs, out_specs=out_specs, check_vma=False)
```

```python
import jax
import jax.numpy as jnp
import numpy as np
from jax import lax
from jax.experimental import pallas as pl
from jax.experimental.pallas import tpu as pltpu
from jax.sharding import PartitionSpec as P


AXES = ("wide", "narrow")
SITES = 27
RING = 8
PLANE = 32
REST = 16
PROFILE = [float(1.0 + 0.5 * np.cos(2.0 * site)) for site in range(SITES)]
RING_HERE = [16, 17, 18]
PLANE_HERE = [11, 12, 13, 14, 15]
RING_AWAY = [25, 26, 21]
PLANE_AWAY = [19, 20, 22, 23, 24]
F32 = jnp.float32
BF16 = jnp.bfloat16


def device_at(ring, plane):
    x, core, y = plane // 8, plane // 4 % 2, plane % 4
    return ((ring % 4 * 4 + x) * 2 + core) * 8 + ring // 4 * 4 + y


def ring_pairs(shift):
    return [
        (device_at(ring, plane), device_at((ring + shift) % RING, plane))
        for ring in range(RING)
        for plane in range(PLANE)
    ]


PLANE_GROUPS = [[device_at(ring, plane) for plane in range(PLANE)] for ring in range(RING)]


def chances(rate_ref, vector):
    level = 0.004 * (rate_ref[vector].astype(F32) + 1.0)
    return [level * PROFILE[site] for site in range(SITES)]


def pick(chance, sites):
    return [chance[site] for site in sites]


def mix_bits(tiles, chance_of_bit):
    tiles = list(tiles)
    for bit, chance in enumerate(chance_of_bit):
        step = 1 << bit
        for low in range(len(tiles)):
            if low & step:
                continue
            flow = chance * (tiles[low | step] - tiles[low])
            tiles[low] = tiles[low] + flow
            tiles[low | step] = tiles[low | step] - flow
    return tiles


def crossing(size, chance_of_bit):
    row = lax.broadcasted_iota(jnp.int32, (size, size), 0)
    column = lax.broadcasted_iota(jnp.int32, (size, size), 1)
    differ = row ^ column
    product = jnp.ones((size, size), F32)
    for bit, chance in enumerate(chance_of_bit):
        product = product * jnp.where((differ >> bit) & 1 == 0, 1.0 - chance, chance)
    return halves(product)


def halves(values):
    high = values.astype(BF16)
    return high, (values - high.astype(F32)).astype(BF16)


def right_matrix(chance):
    high, low = crossing(128, chance[:7])
    top = jnp.concatenate([high, low], axis=1)
    bottom = jnp.concatenate([high, jnp.zeros_like(low)], axis=1)
    return jnp.concatenate([top, bottom], axis=0)


def left_matrix(chance):
    high, low = crossing(256, pick(chance, [7, 8, 9, 10] + PLANE_AWAY[:4]))
    return jnp.concatenate([high, high, low], axis=1)


def mix_blocks(blocks, left, right, chance):
    stacks = []
    for block in blocks:
        high, low = halves(jnp.concatenate([block[:256], block[256:]], axis=1))
        stacks.append(jnp.concatenate([high, low, high], axis=0))
    mixed = [jnp.dot(left, stack, preferred_element_type=F32) for stack in stacks]
    pairs = []
    for both in mixed:
        flow = chance * (both[:, 128:] - both[:, :128])
        tall = jnp.concatenate([both[:, :128] + flow, both[:, 128:] - flow], axis=0)
        pairs.append(jnp.concatenate(halves(tall), axis=1))
    mixed = [jnp.dot(pair, right, preferred_element_type=F32) for pair in pairs]
    return [both[:, :128] + both[:, 128:] for both in mixed]


def spread(row, pattern):
    sub = lax.broadcasted_iota(jnp.int32, (8, 128), 0)
    lane = lax.broadcasted_iota(jnp.int32, (8, 128), 1)
    index = 4 * (8 * pattern + sub) + (lane >> 5)
    return jnp.take_along_axis(
        jnp.broadcast_to(row, (8, 128)), index, axis=1, mode="promise_in_bounds"
    )


def mix_ring(held, chance):
    @pl.loop(0, PLANE, unroll=2)
    def _(plane):
        for half in range(2):
            rows = pl.ds(8 * half, 8)
            mixed = mix_bits([held[ring, plane, rows, :] for ring in range(RING)], chance)
            for ring in range(RING):
                held[ring, plane, rows, :] = mixed[ring]


def mix_plane(held, ring, chance):
    for half in range(2):
        rows = pl.ds(8 * half, 8)
        mixed = mix_bits([held[ring, plane, rows, :] for plane in range(PLANE)], chance)
        for plane in range(PLANE):
            held[ring, plane, rows, :] = mixed[plane]


def my_ring():
    return lax.axis_index("narrow") // 4 * 4 + lax.axis_index("wide") // 8


def ring_slot(shift):
    return lax.rem(my_ring() + shift + RING, RING)


def from_ring(refs, held, sems):
    def copies():
        return [
            pltpu.make_async_copy(ref, held.at[ring_slot(-shift)], sems.at[shift])
            for shift, ref in enumerate(refs)
        ]

    return copies


def to_ring(held, refs, sems):
    def copies():
        return [
            pltpu.make_async_copy(held.at[ring_slot(shift)], ref, sems.at[shift])
            for shift, ref in enumerate(refs)
        ]

    return copies


def plane_copy(ref, held, ring, sems, outward=False):
    rows = pl.ds(pl.multiple_of(REST * ring, REST), REST)
    here, there = held.at[ring], ref.at[:, rows, :]
    if outward:
        return pltpu.make_async_copy(here, there, sems.at[ring])
    return pltpu.make_async_copy(there, here, sems.at[ring])


def start_all(copies):
    for copy in copies:
        copy.start()


def wait_all(copies):
    for copy in copies:
        copy.wait()


def begin_ring(rate_ref, class_ref, x_ref, *refs):
    outs, (x_held, class_held, held, rows_held, in_sems, out_sems, class_sem, rows_sems) = refs[:RING], refs[RING:]
    chance = chances(rate_ref, 0)

    def load(part):
        rows = pl.ds(pl.multiple_of(128 * part, 128), 128)
        return pltpu.make_async_copy(
            x_ref.at[:, rows, :], x_held.at[:, rows, :], in_sems.at[part]
        )

    def send(shift, part):
        planes = pl.ds(4 * part, 4)
        return pltpu.make_async_copy(
            held.at[ring_slot(shift), planes], outs[shift].at[planes], out_sems.at[shift, part]
        )

    def send_rows(shift):
        return pltpu.make_async_copy(
            held.at[ring_slot(shift), PLANE], outs[shift].at[PLANE], rows_sems.at[shift]
        )

    classes = pltpu.make_async_copy(class_ref, class_held, class_sem)
    classes.start()
    for part in range(RING):
        load(part).start()
    classes.wait()
    for ring in range(RING):
        fitness = 0.5 + 0.25 * class_held[REST * ring : REST * ring + REST].astype(F32)
        held[ring, PLANE] = fitness
        for part in range(RING):
            rows_held[part, ring, 0:2, :] = fitness[2 * part : 2 * part + 2]
    start_all([send_rows(shift) for shift in range(RING)])

    @pl.loop(0, RING)
    def _(part):
        load(part).wait()
        for at in range(8):
            plane, rows = 4 * part + at // 2, pl.ds(8 * (at % 2), 8)
            tiles = []
            for ring in range(RING):
                row = at // 4
                scale = spread(rows_held[part, ring, row : row + 1, :], at % 4)
                start = pl.multiple_of(128 * part, 128) + 16 * at
                tiles.append(x_held[ring, pl.ds(start, 8, stride=2), :] * scale)
            for ring, tile in enumerate(mix_bits(tiles, pick(chance, RING_HERE))):
                held[ring, plane, rows, :] = tile
        start_all([send(shift, part) for shift in range(RING)])

    @pl.loop(0, RING)
    def _(part):
        wait_all([send(shift, part) for shift in range(RING)])

    wait_all([send_rows(shift) for shift in range(RING)])


def begin_plane(rate_ref, class_ref, x_ref, out_ref, x_held, class_held, held, in_sems, out_sems, class_sem):
    chance = chances(rate_ref, 1)

    def load(ring):
        return pltpu.make_async_copy(x_ref.at[ring], x_held.at[ring], in_sems.at[ring])

    classes = pltpu.make_async_copy(class_ref, class_held, class_sem)
    classes.start()
    for ring in range(RING):
        load(ring).start()
    classes.wait()

    @pl.loop(0, RING)
    def _(ring):
        load(ring).wait()
        first_row = pl.multiple_of(REST * ring, REST)
        fitness = 0.5 + 0.25 * class_held[pl.ds(first_row, REST), :].astype(F32)
        for half in range(2):
            tiles = []
            for plane in range(PLANE):
                scale = spread(fitness[plane // 2 : plane // 2 + 1], plane % 2 * 2 + half)
                tiles.append(x_held[ring, pl.ds(32 * plane + 16 * half + 1, 8, stride=2), :] * scale)
            for plane, tile in enumerate(mix_bits(tiles, pick(chance, PLANE_HERE))):
                held[ring, plane, pl.ds(8 * half, 8), :] = tile
        plane_copy(out_ref, held, ring, out_sems, outward=True).start()

    wait_all([plane_copy(out_ref, held, ring, out_sems, outward=True) for ring in range(RING)])


def ring_to_plane_first(rate_ref, *refs):
    parts, out_ref, (held, rows_held, in_sems, out_sems, row_sem) = refs[:RING], refs[RING], refs[RING + 1 :]
    chance = chances(rate_ref, 0)
    copies = from_ring(parts, held, in_sems)()
    start_all(copies)
    wait_all(copies)
    for ring in range(RING):
        straight = held[ring, PLANE]
        turned = pltpu.roll(straight, 64, 1)
        for pair in range(REST):
            rows_held[2 * pair, ring : ring + 1, :] = straight[pair : pair + 1]
            rows_held[2 * pair + 1, ring : ring + 1, :] = turned[pair : pair + 1]
    rows_copy = pltpu.make_async_copy(rows_held, out_ref.at[:, pl.ds(RING * REST, RING), :], row_sem)
    rows_copy.start()
    mix_ring(held, pick(chance, RING_AWAY))

    def send(ring):
        return plane_copy(out_ref, held.at[:, pl.ds(0, PLANE)], ring, out_sems, outward=True)

    @pl.loop(0, RING)
    def _(ring):
        mix_plane(held, ring, pick(chance, PLANE_HERE))
        send(ring).start()

    wait_all([send(ring) for ring in range(RING)])
    rows_copy.wait()


TOGETHER = 2


def apply_middle(held, rows_held, first_ring, chance, left_ref, right_ref):
    left, right, across = left_ref[...], right_ref[...], chance[PLANE_AWAY[4]]
    rings = [first_ring + at for at in range(TOGETHER)]
    blocks = [held[ring].reshape(PLANE * REST, 128) for ring in rings]
    blocks = mix_blocks(blocks, left, right, across)
    scaled = []
    for ring, block in zip(rings, blocks):
        tiles = []
        for at in range(2 * PLANE):
            scale = spread(rows_held[at // 2, pl.ds(ring, 1), :], at % 2)
            tiles.append(block[8 * at : 8 * at + 8] * scale)
        scaled.append(jnp.concatenate(tiles, axis=0))
    blocks = mix_blocks(scaled, left, right, across)
    for ring, block in zip(rings, blocks):
        held[ring] = block.reshape(PLANE, REST, 128)


def middle_ring(rate_ref, x_ref, *refs):
    outs, (held, rows_held, left, right, in_sems, out_sems, row_sem) = refs[:RING], refs[RING:]
    chance = chances(rate_ref, 0)
    rows_copy = pltpu.make_async_copy(x_ref.at[:, pl.ds(RING * REST, RING), :], rows_held, row_sem)
    rows_copy.start()
    start_all([plane_copy(x_ref, held, ring, in_sems) for ring in range(RING)])
    left[...] = left_matrix(chance)
    right[...] = right_matrix(chance)
    rows_copy.wait()

    @pl.loop(0, RING, step=TOGETHER)
    def _(ring):
        for at in range(TOGETHER):
            plane_copy(x_ref, held, ring + at, in_sems).wait()
        apply_middle(held, rows_held, ring, chance, left, right)

    mix_ring(held, pick(chance, RING_AWAY))
    copies = to_ring(held, outs, out_sems)()
    start_all(copies)
    wait_all(copies)


def ring_to_plane(rate_ref, *refs):
    parts, out_ref, (held, in_sems, out_sems) = refs[:RING], refs[RING], refs[RING + 1 :]
    chance = chances(rate_ref, 0)
    copies = from_ring(parts, held, in_sems)()
    start_all(copies)
    wait_all(copies)
    mix_ring(held, pick(chance, RING_HERE))
    copies = [plane_copy(out_ref, held, ring, out_sems, outward=True) for ring in range(RING)]
    start_all(copies)
    wait_all(copies)


def end_plane(rate_ref, x_ref, out_ref, held, in_sems, out_sems):
    chance = chances(rate_ref, 0)
    start_all([plane_copy(x_ref, held, ring, in_sems) for ring in range(RING)])

    def send(ring):
        return pltpu.make_async_copy(held.at[ring], out_ref.at[ring], out_sems.at[ring])

    @pl.loop(0, RING)
    def _(ring):
        plane_copy(x_ref, held, ring, in_sems).wait()
        mix_plane(held, ring, pick(chance, PLANE_HERE))
        send(ring).start()

    wait_all([send(ring) for ring in range(RING)])


def plane_to_ring(plane_sites, ring_sites):
    def kernel(rate_ref, x_ref, *refs):
        outs, (held, in_sems, out_sems) = refs[:RING], refs[RING:]
        chance = chances(rate_ref, 1)
        start_all([plane_copy(x_ref, held, ring, in_sems) for ring in range(RING)])

        if plane_sites:

            @pl.loop(0, RING)
            def _(ring):
                plane_copy(x_ref, held, ring, in_sems).wait()
                mix_plane(held, ring, pick(chance, plane_sites))

        else:
            wait_all([plane_copy(x_ref, held, ring, in_sems) for ring in range(RING)])
        if ring_sites:
            mix_ring(held, pick(chance, ring_sites))
        copies = to_ring(held, outs, out_sems)()
        start_all(copies)
        wait_all(copies)

    return kernel


def middle_plane(rate_ref, fitness_ref, *refs):
    parts, out_ref, (held, rows_held, left, right, in_sems, out_sems, row_sem) = refs[:RING], refs[RING], refs[RING + 1 :]
    chance = chances(rate_ref, 1)
    rows_copy = pltpu.make_async_copy(fitness_ref.at[:, pl.ds(RING * REST, RING), :], rows_held, row_sem)
    rows_copy.start()
    copies = from_ring(parts, held, in_sems)()
    start_all(copies)
    left[...] = left_matrix(chance)
    right[...] = right_matrix(chance)
    rows_copy.wait()
    wait_all(copies)
    mix_ring(held, pick(chance, RING_AWAY))

    @pl.loop(0, RING, step=TOGETHER)
    def _(ring):
        apply_middle(held, rows_held, ring, chance, left, right)

    mix_ring(held, pick(chance, RING_AWAY))
    copies = [plane_copy(out_ref, held, ring, out_sems, outward=True) for ring in range(RING)]
    start_all(copies)
    wait_all(copies)


def end_ring(rate_ref, other_ref, *refs):
    parts, out_ref, (held, other_held, out_held, in_sems, other_sems, out_sems) = refs[:RING], refs[RING], refs[RING + 1 :]
    chance = chances(rate_ref, 1)
    other_copies = [
        pltpu.make_async_copy(other_ref.at[ring], other_held.at[ring], other_sems.at[ring])
        for ring in range(RING)
    ]
    copies = from_ring(parts, held, in_sems)()
    start_all(copies + other_copies)
    wait_all(copies + other_copies)

    def send(part):
        rows = pl.ds(pl.multiple_of(128 * part, 128), 128)
        return pltpu.make_async_copy(
            out_held.at[:, rows, :], out_ref.at[:, rows, :], out_sems.at[part]
        )

    @pl.loop(0, RING)
    def _(part):
        for at in range(8):
            plane, rows = 4 * part + at // 2, pl.ds(8 * (at % 2), 8)
            start = pl.multiple_of(128 * part + 16 * at, 16)
            tiles = [held[ring, plane, rows, :] for ring in range(RING)]
            for ring, tile in enumerate(mix_bits(tiles, pick(chance, RING_HERE))):
                out_held[ring, pl.ds(start, 8, stride=2), :] = other_held[ring, plane, rows, :]
                out_held[ring, pl.ds(start + 1, 8, stride=2), :] = tile
        send(part).start()

    wait_all([send(part) for part in range(RING)])


SMEM = pl.BlockSpec(memory_space=pltpu.SMEM)
ANY = pl.BlockSpec(memory_space=pl.ANY)
HELD = pltpu.VMEM((RING, PLANE, REST, 128), F32)
HELD_MORE = pltpu.VMEM((RING, PLANE + 1, REST, 128), F32)
WHOLE = pltpu.VMEM((RING, 1024, 128), F32)
CLASSES = pltpu.VMEM((128, 128), jnp.int32)
ROWS = pltpu.VMEM((PLANE, RING, 128), F32)
CLASS_ROWS = pltpu.VMEM((RING, RING, 8, 128), F32)
MANY = pltpu.SemaphoreType.DMA((RING, RING))
LEFT = pltpu.VMEM((256, 768), BF16)
RIGHT = pltpu.VMEM((256, 256), BF16)
EIGHT = pltpu.SemaphoreType.DMA((RING,))
ONE = pltpu.SemaphoreType.DMA
SENT_RING = [jax.ShapeDtypeStruct((PLANE, REST, 128), F32)] * RING
SENT_RING_MORE = [jax.ShapeDtypeStruct((PLANE + 1, REST, 128), F32)] * RING
SENT_PLANE = jax.ShapeDtypeStruct((PLANE, RING * REST, 128), F32)
SENT_PLANE_MORE = jax.ShapeDtypeStruct((PLANE, RING * REST + RING, 128), F32)


def call(kernel, name, outs, scratch, rate_index, *operands):
    many = isinstance(outs, list)
    return pl.pallas_call(
        kernel,
        out_shape=outs,
        in_specs=[SMEM] + [ANY] * len(operands),
        out_specs=[ANY] * len(outs) if many else ANY,
        scratch_shapes=scratch,
        cost_estimate=pl.CostEstimate(
            flops=1 << 28, bytes_accessed=8 << 20, transcendentals=0
        ),
        compiler_params=pltpu.CompilerParams(vmem_limit_bytes=(56 if name in ("a1", "b1") else 16) << 20),
    )(rate_index, *operands)


def round_ring(parts):
    return [parts[0]] + [
        lax.ppermute(part, AXES, ring_pairs(shift))
        for shift, part in enumerate(parts)
        if shift
    ]


def in_plane(piece):
    return lax.all_to_all(
        piece, AXES, split_axis=0, concat_axis=0, tiled=True, axis_index_groups=PLANE_GROUPS
    )


def per_device(krylov, fitness_class, rate_index):
    rows = krylov.reshape(2, 4096, 128).transpose(1, 0, 2).reshape(RING, 1024, 128)
    classes = fitness_class.reshape(128, 128)
    rate = rate_index
    begin = [WHOLE, CLASSES]
    ends = [EIGHT, EIGHT]

    a = call(begin_ring, "a1", SENT_RING_MORE, begin + [HELD_MORE, CLASS_ROWS, EIGHT, MANY, ONE, EIGHT], rate, classes, rows)
    a = round_ring(a)
    b = call(begin_plane, "b1", SENT_PLANE, begin + [HELD] + ends + [ONE], rate, classes, rows)
    b = in_plane(b)
    b = call(plane_to_ring([], RING_HERE), "b2", SENT_RING, [HELD] + ends, rate, b)
    b = round_ring(b)
    a = call(ring_to_plane_first, "a2", SENT_PLANE_MORE, [HELD_MORE, ROWS] + ends + [ONE], rate, *a)
    a = in_plane(a)
    fitness = a
    a = call(middle_ring, "a3", SENT_RING, [HELD, ROWS, LEFT, RIGHT] + ends + [ONE], rate, a)
    a = round_ring(a)
    b = call(middle_plane, "b3", SENT_PLANE, [HELD, ROWS, LEFT, RIGHT] + ends + [ONE], rate, fitness, *b)
    b = in_plane(b)
    b = call(plane_to_ring(PLANE_HERE, []), "b4", SENT_RING, [HELD] + ends, rate, b)
    b = round_ring(b)
    a = call(ring_to_plane, "a4", SENT_PLANE, [HELD] + ends, rate, *a)
    a = in_plane(a)
    done = jax.ShapeDtypeStruct((RING, PLANE, REST, 128), F32)
    a = call(end_plane, "a5", done, [HELD] + ends, rate, a)
    whole = jax.ShapeDtypeStruct((RING, 1024, 128), F32)
    result = call(end_ring, "b5", whole, [HELD, HELD, WHOLE, EIGHT] + ends, rate, a, *b)
    return result.reshape(4096, 2, 128).transpose(1, 0, 2).reshape(2, 4096 * 128)


def solution(mesh):
    in_specs = (P(None, AXES), P(AXES), P())
    out_specs = P(None, AXES)
    return jax.shard_map(per_device, mesh=mesh, in_specs=in_specs, out_specs=out_specs, check_vma=False)
```

```python
import jax
import jax.numpy as jnp
import numpy as np
from jax import lax
from jax.experimental import pallas as pl
from jax.experimental.pallas import tpu as pltpu
from jax.sharding import PartitionSpec as P


AXES = ("wide", "narrow")
SITES = 27
RING = 8
PLANE = 32
REST = 16
PROFILE = [float(1.0 + 0.5 * np.cos(2.0 * site)) for site in range(SITES)]
RING_HERE = [16, 17, 18]
PLANE_HERE = [11, 12, 13, 14, 15]
RING_AWAY = [25, 26, 21]
PLANE_AWAY = [19, 20, 22, 23, 24]
F32 = jnp.float32
BF16 = jnp.bfloat16


def device_at(ring, plane):
    x, core, y = plane // 8, plane // 4 % 2, plane % 4
    return ((ring % 4 * 4 + x) * 2 + core) * 8 + ring // 4 * 4 + y


def ring_pairs(shift):
    return [
        (device_at(ring, plane), device_at((ring + shift) % RING, plane))
        for ring in range(RING)
        for plane in range(PLANE)
    ]


PLANE_GROUPS = [[device_at(ring, plane) for plane in range(PLANE)] for ring in range(RING)]


def chances(rate_ref, vector):
    level = 0.004 * (rate_ref[vector].astype(F32) + 1.0)
    return [level * PROFILE[site] for site in range(SITES)]


def pick(chance, sites):
    return [chance[site] for site in sites]


def mix_bits(tiles, chance_of_bit):
    tiles = list(tiles)
    for bit, chance in enumerate(chance_of_bit):
        step = 1 << bit
        for low in range(len(tiles)):
            if low & step:
                continue
            flow = chance * (tiles[low | step] - tiles[low])
            tiles[low] = tiles[low] + flow
            tiles[low | step] = tiles[low | step] - flow
    return tiles


def crossing(size, chance_of_bit):
    row = lax.broadcasted_iota(jnp.int32, (size, size), 0)
    column = lax.broadcasted_iota(jnp.int32, (size, size), 1)
    differ = row ^ column
    product = jnp.ones((size, size), F32)
    for bit, chance in enumerate(chance_of_bit):
        product = product * jnp.where((differ >> bit) & 1 == 0, 1.0 - chance, chance)
    return halves(product)


def halves(values):
    high = values.astype(BF16)
    return high, (values - high.astype(F32)).astype(BF16)


def right_matrix(chance):
    high, low = crossing(128, chance[:7])
    top = jnp.concatenate([high, low], axis=1)
    bottom = jnp.concatenate([high, jnp.zeros_like(low)], axis=1)
    return jnp.concatenate([top, bottom], axis=0)


def left_matrix(chance):
    high, low = crossing(256, pick(chance, [7, 8, 9, 10] + PLANE_AWAY[:4]))
    return jnp.concatenate([high, high, low], axis=1)


def mix_blocks(blocks, left, right, chance):
    stacks = []
    for block in blocks:
        high, low = halves(jnp.concatenate([block[:256], block[256:]], axis=1))
        stacks.append(jnp.concatenate([high, low, high], axis=0))
    mixed = [jnp.dot(left, stack, preferred_element_type=F32) for stack in stacks]
    pairs = []
    for both in mixed:
        flow = chance * (both[:, 128:] - both[:, :128])
        tall = jnp.concatenate([both[:, :128] + flow, both[:, 128:] - flow], axis=0)
        pairs.append(jnp.concatenate(halves(tall), axis=1))
    mixed = [jnp.dot(pair, right, preferred_element_type=F32) for pair in pairs]
    return [both[:, :128] + both[:, 128:] for both in mixed]


def spread(row, pattern):
    sub = lax.broadcasted_iota(jnp.int32, (8, 128), 0)
    lane = lax.broadcasted_iota(jnp.int32, (8, 128), 1)
    index = 4 * (8 * pattern + sub) + (lane >> 5)
    return jnp.take_along_axis(
        jnp.broadcast_to(row, (8, 128)), index, axis=1, mode="promise_in_bounds"
    )


def mix_ring(held, chance):
    @pl.loop(0, PLANE, unroll=2)
    def _(plane):
        for half in range(2):
            rows = pl.ds(8 * half, 8)
            mixed = mix_bits([held[ring, plane, rows, :] for ring in range(RING)], chance)
            for ring in range(RING):
                held[ring, plane, rows, :] = mixed[ring]


def mix_plane(held, ring, chance):
    for half in range(2):
        rows = pl.ds(8 * half, 8)
        mixed = mix_bits([held[ring, plane, rows, :] for plane in range(PLANE)], chance)
        for plane in range(PLANE):
            held[ring, plane, rows, :] = mixed[plane]


def my_ring():
    return lax.axis_index("narrow") // 4 * 4 + lax.axis_index("wide") // 8


def ring_slot(shift):
    return lax.rem(my_ring() + shift + RING, RING)


def from_ring(refs, held, sems):
    def copies():
        return [
            pltpu.make_async_copy(ref, held.at[ring_slot(-shift)], sems.at[shift])
            for shift, ref in enumerate(refs)
        ]

    return copies


def to_ring(held, refs, sems):
    def copies():
        return [
            pltpu.make_async_copy(held.at[ring_slot(shift)], ref, sems.at[shift])
            for shift, ref in enumerate(refs)
        ]

    return copies


def plane_copy(ref, held, ring, sems, outward=False):
    rows = pl.ds(pl.multiple_of(REST * ring, REST), REST)
    here, there = held.at[ring], ref.at[:, rows, :]
    if outward:
        return pltpu.make_async_copy(here, there, sems.at[ring])
    return pltpu.make_async_copy(there, here, sems.at[ring])


def start_all(copies):
    for copy in copies:
        copy.start()


def wait_all(copies):
    for copy in copies:
        copy.wait()


def begin_ring(rate_ref, class_ref, x_ref, *refs):
    outs, (x_held, class_held, held, rows_held, in_sems, out_sems, class_sem, rows_sems) = refs[:RING], refs[RING:]
    chance = chances(rate_ref, 0)

    def load(part):
        rows = pl.ds(pl.multiple_of(128 * part, 128), 128)
        return pltpu.make_async_copy(
            x_ref.at[:, rows, :], x_held.at[:, rows, :], in_sems.at[part]
        )

    def send(shift, part):
        planes = pl.ds(4 * part, 4)
        return pltpu.make_async_copy(
            held.at[ring_slot(shift), planes], outs[shift].at[planes], out_sems.at[shift, part]
        )

    def send_rows(shift):
        return pltpu.make_async_copy(
            held.at[ring_slot(shift), PLANE], outs[shift].at[PLANE], rows_sems.at[shift]
        )

    classes = pltpu.make_async_copy(class_ref, class_held, class_sem)
    classes.start()
    for part in range(RING):
        load(part).start()
    classes.wait()
    for ring in range(RING):
        fitness = 0.5 + 0.25 * class_held[REST * ring : REST * ring + REST].astype(F32)
        held[ring, PLANE] = fitness
        for part in range(RING):
            rows_held[part, ring, 0:2, :] = fitness[2 * part : 2 * part + 2]
    start_all([send_rows(shift) for shift in range(RING)])

    @pl.loop(0, RING)
    def _(part):
        load(part).wait()
        for at in range(8):
            plane, rows = 4 * part + at // 2, pl.ds(8 * (at % 2), 8)
            tiles = []
            for ring in range(RING):
                row = at // 4
                scale = spread(rows_held[part, ring, row : row + 1, :], at % 4)
                start = pl.multiple_of(128 * part, 128) + 16 * at
                tiles.append(x_held[ring, pl.ds(start, 8, stride=2), :] * scale)
            for ring, tile in enumerate(mix_bits(tiles, pick(chance, RING_HERE))):
                held[ring, plane, rows, :] = tile
        start_all([send(shift, part) for shift in range(RING)])

    @pl.loop(0, RING)
    def _(part):
        wait_all([send(shift, part) for shift in range(RING)])

    wait_all([send_rows(shift) for shift in range(RING)])


def begin_plane(rate_ref, class_ref, x_ref, out_ref, x_held, class_held, held, in_sems, out_sems, class_sem):
    chance = chances(rate_ref, 1)

    def load(ring):
        return pltpu.make_async_copy(x_ref.at[ring], x_held.at[ring], in_sems.at[ring])

    classes = pltpu.make_async_copy(class_ref, class_held, class_sem)
    classes.start()
    for ring in range(RING):
        load(ring).start()
    classes.wait()

    @pl.loop(0, RING)
    def _(ring):
        load(ring).wait()
        first_row = pl.multiple_of(REST * ring, REST)
        fitness = 0.5 + 0.25 * class_held[pl.ds(first_row, REST), :].astype(F32)
        for half in range(2):
            tiles = []
            for plane in range(PLANE):
                scale = spread(fitness[plane // 2 : plane // 2 + 1], plane % 2 * 2 + half)
                tiles.append(x_held[ring, pl.ds(32 * plane + 16 * half + 1, 8, stride=2), :] * scale)
            for plane, tile in enumerate(mix_bits(tiles, pick(chance, PLANE_HERE))):
                held[ring, plane, pl.ds(8 * half, 8), :] = tile
        plane_copy(out_ref, held, ring, out_sems, outward=True).start()

    wait_all([plane_copy(out_ref, held, ring, out_sems, outward=True) for ring in range(RING)])


def ring_to_plane_first(rate_ref, *refs):
    parts, out_ref, (held, rows_held, in_sems, out_sems, row_sem) = refs[:RING], refs[RING], refs[RING + 1 :]
    chance = chances(rate_ref, 0)
    copies = from_ring(parts, held, in_sems)()
    start_all(copies)
    wait_all(copies)
    for ring in range(RING):
        straight = held[ring, PLANE]
        turned = pltpu.roll(straight, 64, 1)
        for pair in range(REST):
            rows_held[2 * pair, ring : ring + 1, :] = straight[pair : pair + 1]
            rows_held[2 * pair + 1, ring : ring + 1, :] = turned[pair : pair + 1]
    rows_copy = pltpu.make_async_copy(rows_held, out_ref.at[:, pl.ds(RING * REST, RING), :], row_sem)
    rows_copy.start()
    mix_ring(held, pick(chance, RING_AWAY))

    def send(ring):
        return plane_copy(out_ref, held.at[:, pl.ds(0, PLANE)], ring, out_sems, outward=True)

    @pl.loop(0, RING)
    def _(ring):
        mix_plane(held, ring, pick(chance, PLANE_HERE))
        send(ring).start()

    wait_all([send(ring) for ring in range(RING)])
    rows_copy.wait()


TOGETHER = 2


def apply_middle(held, rows_held, first_ring, chance, left_ref, right_ref):
    left, right, across = left_ref[...], right_ref[...], chance[PLANE_AWAY[4]]
    rings = [first_ring + at for at in range(TOGETHER)]
    blocks = [held[ring].reshape(PLANE * REST, 128) for ring in rings]
    blocks = mix_blocks(blocks, left, right, across)
    scaled = []
    for ring, block in zip(rings, blocks):
        tiles = []
        for at in range(2 * PLANE):
            scale = spread(rows_held[at // 2, pl.ds(ring, 1), :], at % 2)
            tiles.append(block[8 * at : 8 * at + 8] * scale)
        scaled.append(jnp.concatenate(tiles, axis=0))
    blocks = mix_blocks(scaled, left, right, across)
    for ring, block in zip(rings, blocks):
        held[ring] = block.reshape(PLANE, REST, 128)


def middle_ring(rate_ref, x_ref, *refs):
    outs, (held, rows_held, left, right, in_sems, out_sems, row_sem) = refs[:RING], refs[RING:]
    chance = chances(rate_ref, 0)
    rows_copy = pltpu.make_async_copy(x_ref.at[:, pl.ds(RING * REST, RING), :], rows_held, row_sem)
    rows_copy.start()
    start_all([plane_copy(x_ref, held, ring, in_sems) for ring in range(RING)])
    left[...] = left_matrix(chance)
    right[...] = right_matrix(chance)
    rows_copy.wait()

    @pl.loop(0, RING, step=TOGETHER)
    def _(ring):
        for at in range(TOGETHER):
            plane_copy(x_ref, held, ring + at, in_sems).wait()
        apply_middle(held, rows_held, ring, chance, left, right)

    mix_ring(held, pick(chance, RING_AWAY))
    copies = to_ring(held, outs, out_sems)()
    start_all(copies)
    wait_all(copies)


def ring_to_plane(rate_ref, *refs):
    parts, out_ref, (held, in_sems, out_sems) = refs[:RING], refs[RING], refs[RING + 1 :]
    chance = chances(rate_ref, 0)
    copies = from_ring(parts, held, in_sems)()
    start_all(copies)
    wait_all(copies)
    mix_ring(held, pick(chance, RING_HERE))
    copies = [plane_copy(out_ref, held, ring, out_sems, outward=True) for ring in range(RING)]
    start_all(copies)
    wait_all(copies)


def end_plane(rate_ref, x_ref, out_ref, held, in_sems, out_sems):
    chance = chances(rate_ref, 0)
    start_all([plane_copy(x_ref, held, ring, in_sems) for ring in range(RING)])

    def send(ring):
        return pltpu.make_async_copy(held.at[ring], out_ref.at[ring], out_sems.at[ring])

    @pl.loop(0, RING)
    def _(ring):
        plane_copy(x_ref, held, ring, in_sems).wait()
        mix_plane(held, ring, pick(chance, PLANE_HERE))
        send(ring).start()

    wait_all([send(ring) for ring in range(RING)])


def plane_to_ring(plane_sites, ring_sites):
    def kernel(rate_ref, x_ref, *refs):
        outs, (held, in_sems, out_sems) = refs[:RING], refs[RING:]
        chance = chances(rate_ref, 1)
        start_all([plane_copy(x_ref, held, ring, in_sems) for ring in range(RING)])

        if plane_sites:

            @pl.loop(0, RING)
            def _(ring):
                plane_copy(x_ref, held, ring, in_sems).wait()
                mix_plane(held, ring, pick(chance, plane_sites))

        else:
            wait_all([plane_copy(x_ref, held, ring, in_sems) for ring in range(RING)])
        if ring_sites:
            mix_ring(held, pick(chance, ring_sites))
        copies = to_ring(held, outs, out_sems)()
        start_all(copies)
        wait_all(copies)

    return kernel


def middle_plane(rate_ref, fitness_ref, *refs):
    parts, out_ref, (held, rows_held, left, right, in_sems, out_sems, row_sem) = refs[:RING], refs[RING], refs[RING + 1 :]
    chance = chances(rate_ref, 1)
    rows_copy = pltpu.make_async_copy(fitness_ref.at[:, pl.ds(RING * REST, RING), :], rows_held, row_sem)
    rows_copy.start()
    copies = from_ring(parts, held, in_sems)()
    start_all(copies)
    left[...] = left_matrix(chance)
    right[...] = right_matrix(chance)
    rows_copy.wait()
    wait_all(copies)
    mix_ring(held, pick(chance, RING_AWAY))

    @pl.loop(0, RING, step=TOGETHER)
    def _(ring):
        apply_middle(held, rows_held, ring, chance, left, right)

    mix_ring(held, pick(chance, RING_AWAY))
    copies = [plane_copy(out_ref, held, ring, out_sems, outward=True) for ring in range(RING)]
    start_all(copies)
    wait_all(copies)


def end_ring(rate_ref, other_ref, *refs):
    parts, out_ref, (held, other_held, out_held, in_sems, other_sems, out_sems) = refs[:RING], refs[RING], refs[RING + 1 :]
    chance = chances(rate_ref, 1)
    other_copies = [
        pltpu.make_async_copy(other_ref.at[ring], other_held.at[ring], other_sems.at[ring])
        for ring in range(RING)
    ]
    copies = from_ring(parts, held, in_sems)()
    start_all(copies + other_copies)
    wait_all(copies + other_copies)

    def send(part):
        rows = pl.ds(pl.multiple_of(128 * part, 128), 128)
        return pltpu.make_async_copy(
            out_held.at[:, rows, :], out_ref.at[:, rows, :], out_sems.at[part]
        )

    @pl.loop(0, RING)
    def _(part):
        for at in range(8):
            plane, rows = 4 * part + at // 2, pl.ds(8 * (at % 2), 8)
            start = pl.multiple_of(128 * part + 16 * at, 16)
            tiles = [held[ring, plane, rows, :] for ring in range(RING)]
            for ring, tile in enumerate(mix_bits(tiles, pick(chance, RING_HERE))):
                out_held[ring, pl.ds(start, 8, stride=2), :] = other_held[ring, plane, rows, :]
                out_held[ring, pl.ds(start + 1, 8, stride=2), :] = tile
        send(part).start()

    wait_all([send(part) for part in range(RING)])


SMEM = pl.BlockSpec(memory_space=pltpu.SMEM)
ANY = pl.BlockSpec(memory_space=pl.ANY)
HELD = pltpu.VMEM((RING, PLANE, REST, 128), F32)
HELD_MORE = pltpu.VMEM((RING, PLANE + 1, REST, 128), F32)
WHOLE = pltpu.VMEM((RING, 1024, 128), F32)
CLASSES = pltpu.VMEM((128, 128), jnp.int32)
ROWS = pltpu.VMEM((PLANE, RING, 128), F32)
CLASS_ROWS = pltpu.VMEM((RING, RING, 8, 128), F32)
MANY = pltpu.SemaphoreType.DMA((RING, RING))
LEFT = pltpu.VMEM((256, 768), BF16)
RIGHT = pltpu.VMEM((256, 256), BF16)
EIGHT = pltpu.SemaphoreType.DMA((RING,))
ONE = pltpu.SemaphoreType.DMA
SENT_RING = [jax.ShapeDtypeStruct((PLANE, REST, 128), F32)] * RING
SENT_RING_MORE = [jax.ShapeDtypeStruct((PLANE + 1, REST, 128), F32)] * RING
SENT_PLANE = jax.ShapeDtypeStruct((PLANE, RING * REST, 128), F32)
SENT_PLANE_MORE = jax.ShapeDtypeStruct((PLANE, RING * REST + RING, 128), F32)


def call(kernel, name, outs, scratch, rate_index, *operands):
    many = isinstance(outs, list)
    return pl.pallas_call(
        kernel,
        out_shape=outs,
        in_specs=[SMEM] + [ANY] * len(operands),
        out_specs=[ANY] * len(outs) if many else ANY,
        scratch_shapes=scratch,
        cost_estimate=pl.CostEstimate(
            flops=1 << 28, bytes_accessed=8 << 20, transcendentals=0
        ),
        compiler_params=pltpu.CompilerParams(vmem_limit_bytes=(56 if name in ("a1", "b1") else 16) << 20),
    )(rate_index, *operands)


SOONER = (3, 5)


def round_ring(parts):
    moved = list(parts)
    for shifts in (SOONER, [shift for shift in range(1, RING) if shift not in SOONER]):
        for shift in shifts:
            moved[shift] = lax.ppermute(parts[shift], AXES, ring_pairs(shift))
    return moved


def in_plane(piece):
    return lax.all_to_all(
        piece, AXES, split_axis=0, concat_axis=0, tiled=True, axis_index_groups=PLANE_GROUPS
    )


def per_device(krylov, fitness_class, rate_index):
    rows = krylov.reshape(2, 4096, 128).transpose(1, 0, 2).reshape(RING, 1024, 128)
    classes = fitness_class.reshape(128, 128)
    rate = rate_index
    begin = [WHOLE, CLASSES]
    ends = [EIGHT, EIGHT]

    a = call(begin_ring, "a1", SENT_RING_MORE, begin + [HELD_MORE, CLASS_ROWS, EIGHT, MANY, ONE, EIGHT], rate, classes, rows)
    a = round_ring(a)
    b = call(begin_plane, "b1", SENT_PLANE, begin + [HELD] + ends + [ONE], rate, classes, rows)
    b = in_plane(b)
    b = call(plane_to_ring([], RING_HERE), "b2", SENT_RING, [HELD] + ends, rate, b)
    b = round_ring(b)
    a = call(ring_to_plane_first, "a2", SENT_PLANE_MORE, [HELD_MORE, ROWS] + ends + [ONE], rate, *a)
    a = in_plane(a)
    fitness = a
    a = call(middle_ring, "a3", SENT_RING, [HELD, ROWS, LEFT, RIGHT] + ends + [ONE], rate, a)
    a = round_ring(a)
    b = call(middle_plane, "b3", SENT_PLANE, [HELD, ROWS, LEFT, RIGHT] + ends + [ONE], rate, fitness, *b)
    b = in_plane(b)
    b = call(plane_to_ring(PLANE_HERE, []), "b4", SENT_RING, [HELD] + ends, rate, b)
    b = round_ring(b)
    a = call(ring_to_plane, "a4", SENT_PLANE, [HELD] + ends, rate, *a)
    a = in_plane(a)
    done = jax.ShapeDtypeStruct((RING, PLANE, REST, 128), F32)
    a = call(end_plane, "a5", done, [HELD] + ends, rate, a)
    whole = jax.ShapeDtypeStruct((RING, 1024, 128), F32)
    result = call(end_ring, "b5", whole, [HELD, HELD, WHOLE, EIGHT] + ends, rate, a, *b)
    return result.reshape(4096, 2, 128).transpose(1, 0, 2).reshape(2, 4096 * 128)


def solution(mesh):
    in_specs = (P(None, AXES), P(AXES), P())
    out_specs = P(None, AXES)
    return jax.shard_map(per_device, mesh=mesh, in_specs=in_specs, out_specs=out_specs, check_vma=False)
```

```python
import jax
import jax.numpy as jnp
import numpy as np
from jax import lax
from jax.experimental import pallas as pl
from jax.experimental.pallas import tpu as pltpu
from jax.sharding import PartitionSpec as P


AXES = ("wide", "narrow")
SITES = 27
RING = 8
PLANE = 32
REST = 16
PROFILE = [float(1.0 + 0.5 * np.cos(2.0 * site)) for site in range(SITES)]
RING_HERE = [16, 17, 18]
PLANE_HERE = [11, 12, 13, 14, 15]
RING_AWAY = [25, 26, 21]
PLANE_AWAY = [19, 20, 22, 23, 24]
F32 = jnp.float32
BF16 = jnp.bfloat16


def device_at(ring, plane):
    x, core, y = plane // 8, plane // 4 % 2, plane % 4
    return ((ring % 4 * 4 + x) * 2 + core) * 8 + ring // 4 * 4 + y


def ring_pairs(shift):
    return [
        (device_at(ring, plane), device_at((ring + shift) % RING, plane))
        for ring in range(RING)
        for plane in range(PLANE)
    ]


PLANE_GROUPS = [[device_at(ring, plane) for plane in range(PLANE)] for ring in range(RING)]


def chances(rate_ref, vector):
    level = 0.004 * (rate_ref[vector].astype(F32) + 1.0)
    return [level * PROFILE[site] for site in range(SITES)]


def pick(chance, sites):
    return [chance[site] for site in sites]


def mix_bits(tiles, chance_of_bit):
    tiles = list(tiles)
    for bit, chance in enumerate(chance_of_bit):
        step = 1 << bit
        for low in range(len(tiles)):
            if low & step:
                continue
            flow = chance * (tiles[low | step] - tiles[low])
            tiles[low] = tiles[low] + flow
            tiles[low | step] = tiles[low | step] - flow
    return tiles


def crossing(size, chance_of_bit):
    row = lax.broadcasted_iota(jnp.int32, (size, size), 0)
    column = lax.broadcasted_iota(jnp.int32, (size, size), 1)
    differ = row ^ column
    product = jnp.ones((size, size), F32)
    for bit, chance in enumerate(chance_of_bit):
        product = product * jnp.where((differ >> bit) & 1 == 0, 1.0 - chance, chance)
    return halves(product)


def halves(values):
    high = values.astype(BF16)
    return high, (values - high.astype(F32)).astype(BF16)


def right_matrix(chance):
    high, low = crossing(128, chance[:7])
    top = jnp.concatenate([high, low], axis=1)
    bottom = jnp.concatenate([high, jnp.zeros_like(low)], axis=1)
    return jnp.concatenate([top, bottom], axis=0)


def left_matrix(chance):
    high, low = crossing(256, pick(chance, [7, 8, 9, 10] + PLANE_AWAY[:4]))
    return jnp.concatenate([high, high, low], axis=1)


def mix_blocks(blocks, left, right, chance):
    stacks = []
    for block in blocks:
        high, low = halves(jnp.concatenate([block[:256], block[256:]], axis=1))
        stacks.append(jnp.concatenate([high, low, high], axis=0))
    mixed = [jnp.dot(left, stack, preferred_element_type=F32) for stack in stacks]
    pairs = []
    for both in mixed:
        flow = chance * (both[:, 128:] - both[:, :128])
        tall = jnp.concatenate([both[:, :128] + flow, both[:, 128:] - flow], axis=0)
        pairs.append(jnp.concatenate(halves(tall), axis=1))
    mixed = [jnp.dot(pair, right, preferred_element_type=F32) for pair in pairs]
    return [both[:, :128] + both[:, 128:] for both in mixed]


def spread(row, pattern):
    sub = lax.broadcasted_iota(jnp.int32, (8, 128), 0)
    lane = lax.broadcasted_iota(jnp.int32, (8, 128), 1)
    index = 4 * (8 * pattern + sub) + (lane >> 5)
    return jnp.take_along_axis(
        jnp.broadcast_to(row, (8, 128)), index, axis=1, mode="promise_in_bounds"
    )


PARTS = 4
PART = PLANE // PARTS


def mix_ring(held, chance, sends=None):
    @pl.loop(0, PARTS)
    def _(part):
        for at in range(PART):
            for half in range(2):
                plane, rows = PART * part + at, pl.ds(8 * half, 8)
                mixed = mix_bits([held[ring, plane, rows, :] for ring in range(RING)], chance)
                for ring in range(RING):
                    held[ring, plane, rows, :] = mixed[ring]
        if sends:
            start_all(sends(part))

    if sends:

        @pl.loop(0, PARTS)
        def _(part):
            wait_all(sends(part))


def mix_plane(held, ring, chance):
    for half in range(2):
        rows = pl.ds(8 * half, 8)
        mixed = mix_bits([held[ring, plane, rows, :] for plane in range(PLANE)], chance)
        for plane in range(PLANE):
            held[ring, plane, rows, :] = mixed[plane]


def my_ring():
    return lax.axis_index("narrow") // 4 * 4 + lax.axis_index("wide") // 8


def ring_slot(shift):
    return lax.rem(my_ring() + shift + RING, RING)


def from_ring(refs, held, sems):
    def copies():
        return [
            pltpu.make_async_copy(ref, held.at[ring_slot(-shift)], sems.at[shift])
            for shift, ref in enumerate(refs)
        ]

    return copies


def to_ring(held, refs, sems):
    def copies(part):
        planes = pl.ds(PART * part, PART)
        return [
            pltpu.make_async_copy(
                held.at[ring_slot(shift), planes], ref.at[planes], sems.at[shift, part]
            )
            for shift, ref in enumerate(refs)
        ]

    return copies


def to_plane(held, ref, sems):
    def copies(part):
        planes = pl.ds(PART * part, PART)
        return [
            pltpu.make_async_copy(
                held.at[ring, planes],
                ref.at[planes, pl.ds(REST * ring, REST), :],
                sems.at[ring, part],
            )
            for ring in range(RING)
        ]

    return copies


def plane_copy(ref, held, ring, sems, outward=False):
    rows = pl.ds(pl.multiple_of(REST * ring, REST), REST)
    here, there = held.at[ring], ref.at[:, rows, :]
    if outward:
        return pltpu.make_async_copy(here, there, sems.at[ring])
    return pltpu.make_async_copy(there, here, sems.at[ring])


def start_all(copies):
    for copy in copies:
        copy.start()


def wait_all(copies):
    for copy in copies:
        copy.wait()


def begin_ring(rate_ref, class_ref, x_ref, *refs):
    outs, (x_held, class_held, held, rows_held, in_sems, out_sems, class_sem, rows_sems) = refs[:RING], refs[RING:]
    chance = chances(rate_ref, 0)

    def load(part):
        rows = pl.ds(pl.multiple_of(128 * part, 128), 128)
        return pltpu.make_async_copy(
            x_ref.at[:, rows, :], x_held.at[:, rows, :], in_sems.at[part]
        )

    def send(shift, part):
        planes = pl.ds(4 * part, 4)
        return pltpu.make_async_copy(
            held.at[ring_slot(shift), planes], outs[shift].at[planes], out_sems.at[shift, part]
        )

    def send_rows(shift):
        return pltpu.make_async_copy(
            held.at[ring_slot(shift), PLANE], outs[shift].at[PLANE], rows_sems.at[shift]
        )

    classes = pltpu.make_async_copy(class_ref, class_held, class_sem)
    classes.start()
    for part in range(RING):
        load(part).start()
    classes.wait()
    for ring in range(RING):
        fitness = 0.5 + 0.25 * class_held[REST * ring : REST * ring + REST].astype(F32)
        held[ring, PLANE] = fitness
        for part in range(RING):
            rows_held[part, ring, 0:2, :] = fitness[2 * part : 2 * part + 2]
    start_all([send_rows(shift) for shift in range(RING)])

    @pl.loop(0, RING)
    def _(part):
        load(part).wait()
        for at in range(8):
            plane, rows = 4 * part + at // 2, pl.ds(8 * (at % 2), 8)
            tiles = []
            for ring in range(RING):
                row = at // 4
                scale = spread(rows_held[part, ring, row : row + 1, :], at % 4)
                start = pl.multiple_of(128 * part, 128) + 16 * at
                tiles.append(x_held[ring, pl.ds(start, 8, stride=2), :] * scale)
            for ring, tile in enumerate(mix_bits(tiles, pick(chance, RING_HERE))):
                held[ring, plane, rows, :] = tile
        start_all([send(shift, part) for shift in range(RING)])

    @pl.loop(0, RING)
    def _(part):
        wait_all([send(shift, part) for shift in range(RING)])

    wait_all([send_rows(shift) for shift in range(RING)])


def begin_plane(rate_ref, class_ref, x_ref, out_ref, x_held, class_held, held, in_sems, out_sems, class_sem):
    chance = chances(rate_ref, 1)

    def load(ring):
        return pltpu.make_async_copy(x_ref.at[ring], x_held.at[ring], in_sems.at[ring])

    classes = pltpu.make_async_copy(class_ref, class_held, class_sem)
    classes.start()
    for ring in range(RING):
        load(ring).start()
    classes.wait()

    @pl.loop(0, RING)
    def _(ring):
        load(ring).wait()
        first_row = pl.multiple_of(REST * ring, REST)
        fitness = 0.5 + 0.25 * class_held[pl.ds(first_row, REST), :].astype(F32)
        for half in range(2):
            tiles = []
            for plane in range(PLANE):
                scale = spread(fitness[plane // 2 : plane // 2 + 1], plane % 2 * 2 + half)
                tiles.append(x_held[ring, pl.ds(32 * plane + 16 * half + 1, 8, stride=2), :] * scale)
            for plane, tile in enumerate(mix_bits(tiles, pick(chance, PLANE_HERE))):
                held[ring, plane, pl.ds(8 * half, 8), :] = tile
        plane_copy(out_ref, held, ring, out_sems, outward=True).start()

    wait_all([plane_copy(out_ref, held, ring, out_sems, outward=True) for ring in range(RING)])


def ring_to_plane_first(rate_ref, *refs):
    parts, out_ref, (held, rows_held, in_sems, out_sems, row_sem) = refs[:RING], refs[RING], refs[RING + 1 :]
    chance = chances(rate_ref, 0)
    copies = from_ring(parts, held, in_sems)()
    start_all(copies)
    wait_all(copies)
    for ring in range(RING):
        straight = held[ring, PLANE]
        turned = pltpu.roll(straight, 64, 1)
        for pair in range(REST):
            rows_held[2 * pair, ring : ring + 1, :] = straight[pair : pair + 1]
            rows_held[2 * pair + 1, ring : ring + 1, :] = turned[pair : pair + 1]
    rows_copy = pltpu.make_async_copy(rows_held, out_ref.at[:, pl.ds(RING * REST, RING), :], row_sem)
    rows_copy.start()
    mix_ring(held, pick(chance, RING_AWAY))

    def send(ring):
        return plane_copy(out_ref, held.at[:, pl.ds(0, PLANE)], ring, out_sems, outward=True)

    @pl.loop(0, RING)
    def _(ring):
        mix_plane(held, ring, pick(chance, PLANE_HERE))
        send(ring).start()

    wait_all([send(ring) for ring in range(RING)])
    rows_copy.wait()


TOGETHER = 4


def apply_middle(held, rows_held, first_ring, chance, left_ref, right_ref):
    left, right, across = left_ref[...], right_ref[...], chance[PLANE_AWAY[4]]
    rings = [first_ring + at for at in range(TOGETHER)]
    blocks = [held[ring].reshape(PLANE * REST, 128) for ring in rings]
    blocks = mix_blocks(blocks, left, right, across)
    scaled = []
    for ring, block in zip(rings, blocks):
        tiles = []
        for at in range(2 * PLANE):
            scale = spread(rows_held[at // 2, pl.ds(ring, 1), :], at % 2)
            tiles.append(block[8 * at : 8 * at + 8] * scale)
        scaled.append(jnp.concatenate(tiles, axis=0))
    blocks = mix_blocks(scaled, left, right, across)
    for ring, block in zip(rings, blocks):
        held[ring] = block.reshape(PLANE, REST, 128)


def middle_ring(rate_ref, x_ref, *refs):
    outs, (held, rows_held, left, right, in_sems, out_sems, row_sem) = refs[:RING], refs[RING:]
    chance = chances(rate_ref, 0)
    rows_copy = pltpu.make_async_copy(x_ref.at[:, pl.ds(RING * REST, RING), :], rows_held, row_sem)
    rows_copy.start()
    start_all([plane_copy(x_ref, held, ring, in_sems) for ring in range(RING)])
    left[...] = left_matrix(chance)
    right[...] = right_matrix(chance)
    rows_copy.wait()

    @pl.loop(0, RING, step=TOGETHER)
    def _(ring):
        for at in range(TOGETHER):
            plane_copy(x_ref, held, ring + at, in_sems).wait()
        apply_middle(held, rows_held, ring, chance, left, right)

    mix_ring(held, pick(chance, RING_AWAY), to_ring(held, outs, out_sems))


def ring_to_plane(rate_ref, *refs):
    parts, out_ref, (held, in_sems, out_sems) = refs[:RING], refs[RING], refs[RING + 1 :]
    chance = chances(rate_ref, 0)
    copies = from_ring(parts, held, in_sems)()
    start_all(copies)
    wait_all(copies)
    mix_ring(held, pick(chance, RING_HERE), to_plane(held, out_ref, out_sems))


def end_plane(rate_ref, x_ref, out_ref, held, in_sems, out_sems):
    chance = chances(rate_ref, 0)
    start_all([plane_copy(x_ref, held, ring, in_sems) for ring in range(RING)])

    def send(ring):
        return pltpu.make_async_copy(held.at[ring], out_ref.at[ring], out_sems.at[ring])

    @pl.loop(0, RING)
    def _(ring):
        plane_copy(x_ref, held, ring, in_sems).wait()
        mix_plane(held, ring, pick(chance, PLANE_HERE))
        send(ring).start()

    wait_all([send(ring) for ring in range(RING)])


def plane_to_ring_first(rate_ref, x_ref, *refs):
    outs, (held, in_sems, out_sems) = refs[:RING], refs[RING:]
    chance = chances(rate_ref, 1)
    copies = [plane_copy(x_ref, held, ring, in_sems) for ring in range(RING)]
    start_all(copies)
    wait_all(copies)
    mix_ring(held, pick(chance, RING_HERE), to_ring(held, outs, out_sems))


def plane_to_ring(rate_ref, x_ref, *refs):
    outs, (held, in_sems, out_sems) = refs[:RING], refs[RING:]
    chance = chances(rate_ref, 1)
    start_all([plane_copy(x_ref, held, ring, in_sems) for ring in range(RING)])

    def send(shift):
        return pltpu.make_async_copy(
            held.at[ring_slot(shift)], outs[shift], out_sems.at[shift, 0]
        )

    for shift in (3, 5, 2, 6, 1, 4, 7, 0):
        ring = ring_slot(shift)
        plane_copy(x_ref, held, ring, in_sems).wait()
        mix_plane(held, ring, pick(chance, PLANE_HERE))
        send(shift).start()
    wait_all([send(shift) for shift in range(RING)])


def middle_plane(rate_ref, fitness_ref, *refs):
    parts, out_ref, (held, rows_held, left, right, in_sems, out_sems, row_sem) = refs[:RING], refs[RING], refs[RING + 1 :]
    chance = chances(rate_ref, 1)
    rows_copy = pltpu.make_async_copy(fitness_ref.at[:, pl.ds(RING * REST, RING), :], rows_held, row_sem)
    rows_copy.start()
    copies = from_ring(parts, held, in_sems)()
    start_all(copies)
    left[...] = left_matrix(chance)
    right[...] = right_matrix(chance)
    rows_copy.wait()
    wait_all(copies)
    mix_ring(held, pick(chance, RING_AWAY))

    @pl.loop(0, RING, step=TOGETHER)
    def _(ring):
        apply_middle(held, rows_held, ring, chance, left, right)

    mix_ring(held, pick(chance, RING_AWAY), to_plane(held, out_ref, out_sems))


def end_ring(rate_ref, other_ref, *refs):
    parts, out_ref, (held, other_held, out_held, in_sems, other_sems, out_sems) = refs[:RING], refs[RING], refs[RING + 1 :]
    chance = chances(rate_ref, 1)
    other_copies = [
        pltpu.make_async_copy(other_ref.at[ring], other_held.at[ring], other_sems.at[ring])
        for ring in range(RING)
    ]
    copies = from_ring(parts, held, in_sems)()
    start_all(copies + other_copies)
    wait_all(copies + other_copies)

    def send(part):
        rows = pl.ds(pl.multiple_of(128 * part, 128), 128)
        return pltpu.make_async_copy(
            out_held.at[:, rows, :], out_ref.at[:, rows, :], out_sems.at[part]
        )

    @pl.loop(0, RING)
    def _(part):
        for at in range(8):
            plane, rows = 4 * part + at // 2, pl.ds(8 * (at % 2), 8)
            start = pl.multiple_of(128 * part + 16 * at, 16)
            tiles = [held[ring, plane, rows, :] for ring in range(RING)]
            for ring, tile in enumerate(mix_bits(tiles, pick(chance, RING_HERE))):
                out_held[ring, pl.ds(start, 8, stride=2), :] = other_held[ring, plane, rows, :]
                out_held[ring, pl.ds(start + 1, 8, stride=2), :] = tile
        send(part).start()

    wait_all([send(part) for part in range(RING)])


SMEM = pl.BlockSpec(memory_space=pltpu.SMEM)
ANY = pl.BlockSpec(memory_space=pl.ANY)
HELD = pltpu.VMEM((RING, PLANE, REST, 128), F32)
HELD_MORE = pltpu.VMEM((RING, PLANE + 1, REST, 128), F32)
WHOLE = pltpu.VMEM((RING, 1024, 128), F32)
CLASSES = pltpu.VMEM((128, 128), jnp.int32)
ROWS = pltpu.VMEM((PLANE, RING, 128), F32)
CLASS_ROWS = pltpu.VMEM((RING, RING, 8, 128), F32)
MANY = pltpu.SemaphoreType.DMA((RING, RING))
LEFT = pltpu.VMEM((256, 768), BF16)
RIGHT = pltpu.VMEM((256, 256), BF16)
EIGHT = pltpu.SemaphoreType.DMA((RING,))
ONE = pltpu.SemaphoreType.DMA
SENT_RING = [jax.ShapeDtypeStruct((PLANE, REST, 128), F32)] * RING
SENT_RING_MORE = [jax.ShapeDtypeStruct((PLANE + 1, REST, 128), F32)] * RING
SENT_PLANE = jax.ShapeDtypeStruct((PLANE, RING * REST, 128), F32)
SENT_PLANE_MORE = jax.ShapeDtypeStruct((PLANE, RING * REST + RING, 128), F32)


def far(shape):
    return pltpu.HBM(shape.shape, shape.dtype)


def call(kernel, name, outs, scratch, rate_index, *operands):
    many = isinstance(outs, list)
    return pl.pallas_call(
        kernel,
        out_shape=[far(out) for out in outs] if many else outs if name == "a5" else far(outs),
        in_specs=[SMEM] + [ANY] * len(operands),
        out_specs=[ANY] * len(outs) if many else ANY,
        scratch_shapes=scratch,
        cost_estimate=pl.CostEstimate(
            flops=1 << 28, bytes_accessed=8 << 20, transcendentals=0
        ),
        compiler_params=pltpu.CompilerParams(vmem_limit_bytes=(56 if name in ("a1", "b1") else 16) << 20),
    )(rate_index, *operands)


def round_ring(parts, sooner=(3, 5)):
    moved = list(parts)
    for shifts in (sooner, [shift for shift in range(1, RING) if shift not in sooner]):
        for shift in shifts:
            moved[shift] = lax.ppermute(parts[shift], AXES, ring_pairs(shift))
    return moved


def in_plane(piece):
    return lax.all_to_all(
        piece, AXES, split_axis=0, concat_axis=0, tiled=True, axis_index_groups=PLANE_GROUPS
    )


def per_device(krylov, fitness_class, rate_index):
    rows = krylov.reshape(2, 4096, 128).transpose(1, 0, 2).reshape(RING, 1024, 128)
    classes = fitness_class.reshape(128, 128)
    rate = rate_index
    begin = [WHOLE, CLASSES]
    ends = [EIGHT, EIGHT]
    fine = [EIGHT, MANY]

    a = call(begin_ring, "a1", SENT_RING_MORE, begin + [HELD_MORE, CLASS_ROWS, EIGHT, MANY, ONE, EIGHT], rate, classes, rows)
    a = round_ring(a)
    b = call(begin_plane, "b1", SENT_PLANE, begin + [HELD] + ends + [ONE], rate, classes, rows)
    b = in_plane(b)
    b = call(plane_to_ring_first, "b2", SENT_RING, [HELD] + fine, rate, b)
    b = round_ring(b)
    a = call(ring_to_plane_first, "a2", SENT_PLANE_MORE, [HELD_MORE, ROWS] + ends + [ONE], rate, *a)
    a = in_plane(a)
    fitness = a
    a = call(middle_ring, "a3", SENT_RING, [HELD, ROWS, LEFT, RIGHT] + fine + [ONE], rate, a)
    a = round_ring(a)
    b = call(middle_plane, "b3", SENT_PLANE, [HELD, ROWS, LEFT, RIGHT] + fine + [ONE], rate, fitness, *b)
    b = in_plane(b)
    b = call(plane_to_ring, "b4", SENT_RING, [HELD] + fine, rate, b)
    b = round_ring(b, (3, 5, 2, 6))
    a = call(ring_to_plane, "a4", SENT_PLANE, [HELD] + fine, rate, *a)
    a = in_plane(a)
    done = jax.ShapeDtypeStruct((RING, PLANE, REST, 128), F32)
    a = call(end_plane, "a5", done, [HELD] + ends, rate, a)
    whole = jax.ShapeDtypeStruct((RING, 1024, 128), F32)
    result = call(end_ring, "b5", whole, [HELD, HELD, WHOLE, EIGHT] + ends, rate, a, *b)
    return result.reshape(4096, 2, 128).transpose(1, 0, 2).reshape(2, 4096 * 128)


def solution(mesh):
    in_specs = (P(None, AXES), P(AXES), P())
    out_specs = P(None, AXES)
    return jax.shard_map(per_device, mesh=mesh, in_specs=in_specs, out_specs=out_specs, check_vma=False)
```

```python
import jax
import jax.numpy as jnp
import numpy as np
from jax import lax
from jax.experimental import pallas as pl
from jax.experimental.pallas import tpu as pltpu
from jax.sharding import PartitionSpec as P


AXES = ("wide", "narrow")
SITES = 27
RING = 8
PLANE = 32
REST = 16
PROFILE = [float(1.0 + 0.5 * np.cos(2.0 * site)) for site in range(SITES)]
RING_HERE = [16, 17, 18]
PLANE_HERE = [11, 12, 13, 14, 15]
RING_AWAY = [25, 26, 21]
PLANE_AWAY = [19, 20, 22, 23, 24]
F32 = jnp.float32
BF16 = jnp.bfloat16


def device_at(ring, plane):
    x, core, y = plane // 8, plane // 4 % 2, plane % 4
    return ((ring % 4 * 4 + x) * 2 + core) * 8 + ring // 4 * 4 + y


def ring_pairs(shift):
    return [
        (device_at(ring, plane), device_at((ring + shift) % RING, plane))
        for ring in range(RING)
        for plane in range(PLANE)
    ]


PLANE_GROUPS = [[device_at(ring, plane) for plane in range(PLANE)] for ring in range(RING)]


def chances(rate_ref, vector):
    level = 0.004 * (rate_ref[vector].astype(F32) + 1.0)
    return [level * PROFILE[site] for site in range(SITES)]


def pick(chance, sites):
    return [chance[site] for site in sites]


def mix_bits(tiles, chance_of_bit):
    tiles = list(tiles)
    for bit, chance in enumerate(chance_of_bit):
        step = 1 << bit
        for low in range(len(tiles)):
            if low & step:
                continue
            flow = chance * (tiles[low | step] - tiles[low])
            tiles[low] = tiles[low] + flow
            tiles[low | step] = tiles[low | step] - flow
    return tiles


def crossing(size, chance_of_bit):
    row = lax.broadcasted_iota(jnp.int32, (size, size), 0)
    column = lax.broadcasted_iota(jnp.int32, (size, size), 1)
    differ = row ^ column
    product = jnp.ones((size, size), F32)
    for bit, chance in enumerate(chance_of_bit):
        product = product * jnp.where((differ >> bit) & 1 == 0, 1.0 - chance, chance)
    return halves(product)


def halves(values):
    high = values.astype(BF16)
    return high, (values - high.astype(F32)).astype(BF16)


def right_matrix(chance):
    high, low = crossing(128, chance[:7])
    top = jnp.concatenate([high, low], axis=1)
    bottom = jnp.concatenate([high, jnp.zeros_like(low)], axis=1)
    return jnp.concatenate([top, bottom], axis=0)


def left_matrix(chance):
    high, low = crossing(256, pick(chance, [7, 8, 9, 10] + PLANE_AWAY[:4]))
    return jnp.concatenate([high, high, low], axis=1)


def mix_blocks(blocks, left, right, chance):
    stacks = []
    for block in blocks:
        high, low = halves(jnp.concatenate([block[:256], block[256:]], axis=1))
        stacks.append(jnp.concatenate([high, low, high], axis=0))
    mixed = [jnp.dot(left, stack, preferred_element_type=F32) for stack in stacks]
    pairs = []
    for both in mixed:
        flow = chance * (both[:, 128:] - both[:, :128])
        tall = jnp.concatenate([both[:, :128] + flow, both[:, 128:] - flow], axis=0)
        pairs.append(jnp.concatenate(halves(tall), axis=1))
    mixed = [jnp.dot(pair, right, preferred_element_type=F32) for pair in pairs]
    return [both[:, :128] + both[:, 128:] for both in mixed]


def spread(row, pattern):
    sub = lax.broadcasted_iota(jnp.int32, (8, 128), 0)
    lane = lax.broadcasted_iota(jnp.int32, (8, 128), 1)
    index = 4 * (8 * pattern + sub) + (lane >> 5)
    return jnp.take_along_axis(
        jnp.broadcast_to(row, (8, 128)), index, axis=1, mode="promise_in_bounds"
    )


PARTS = 4
PART = PLANE // PARTS


def mix_ring(held, chance, sends=None):
    @pl.loop(0, PARTS)
    def _(part):
        for at in range(PART):
            for half in range(2):
                plane, rows = PART * part + at, pl.ds(8 * half, 8)
                mixed = mix_bits([held[ring, plane, rows, :] for ring in range(RING)], chance)
                for ring in range(RING):
                    held[ring, plane, rows, :] = mixed[ring]
        if sends:
            start_all(sends(part))

    if sends:

        @pl.loop(0, PARTS)
        def _(part):
            wait_all(sends(part))


def mix_plane(held, ring, chance):
    for half in range(2):
        rows = pl.ds(8 * half, 8)
        mixed = mix_bits([held[ring, plane, rows, :] for plane in range(PLANE)], chance)
        for plane in range(PLANE):
            held[ring, plane, rows, :] = mixed[plane]


def my_ring():
    return lax.axis_index("narrow") // 4 * 4 + lax.axis_index("wide") // 8


def ring_slot(shift):
    return lax.rem(my_ring() + shift + RING, RING)


def from_ring(refs, held, sems):
    def copies():
        return [
            pltpu.make_async_copy(ref, held.at[ring_slot(-shift)], sems.at[shift])
            for shift, ref in enumerate(refs)
        ]

    return copies


def to_ring(held, refs, sems):
    def copies(part):
        planes = pl.ds(PART * part, PART)
        return [
            pltpu.make_async_copy(
                held.at[ring_slot(shift), planes], ref.at[planes], sems.at[shift, part]
            )
            for shift, ref in enumerate(refs)
        ]

    return copies


def to_plane(held, ref, sems):
    def copies(part):
        planes = pl.ds(PART * part, PART)
        return [
            pltpu.make_async_copy(
                held.at[ring, planes],
                ref.at[planes, pl.ds(REST * ring, REST), :],
                sems.at[ring, part],
            )
            for ring in range(RING)
        ]

    return copies


def plane_copy(ref, held, ring, sems, outward=False):
    rows = pl.ds(pl.multiple_of(REST * ring, REST), REST)
    here, there = held.at[ring], ref.at[:, rows, :]
    if outward:
        return pltpu.make_async_copy(here, there, sems.at[ring])
    return pltpu.make_async_copy(there, here, sems.at[ring])


def start_all(copies):
    for copy in copies:
        copy.start()


def wait_all(copies):
    for copy in copies:
        copy.wait()


def begin_ring(rate_ref, class_ref, x_ref, *refs):
    outs, (x_held, class_held, held, rows_held, in_sems, out_sems, class_sem, rows_sems) = refs[:RING], refs[RING:]
    chance = chances(rate_ref, 0)

    def load(part):
        rows = pl.ds(pl.multiple_of(128 * part, 128), 128)
        return pltpu.make_async_copy(
            x_ref.at[:, rows, :], x_held.at[:, rows, :], in_sems.at[part]
        )

    def send(shift, part):
        planes = pl.ds(4 * part, 4)
        return pltpu.make_async_copy(
            held.at[ring_slot(shift), planes], outs[shift].at[planes], out_sems.at[shift, part]
        )

    def send_rows(shift):
        return pltpu.make_async_copy(
            held.at[ring_slot(shift), PLANE], outs[shift].at[PLANE], rows_sems.at[shift]
        )

    classes = pltpu.make_async_copy(class_ref, class_held, class_sem)
    classes.start()
    for part in range(RING):
        load(part).start()
    classes.wait()
    for ring in range(RING):
        fitness = 0.5 + 0.25 * class_held[REST * ring : REST * ring + REST].astype(F32)
        held[ring, PLANE] = fitness
        for part in range(RING):
            rows_held[part, ring, 0:2, :] = fitness[2 * part : 2 * part + 2]
    start_all([send_rows(shift) for shift in range(RING)])

    @pl.loop(0, RING)
    def _(part):
        load(part).wait()
        for at in range(8):
            plane, rows = 4 * part + at // 2, pl.ds(8 * (at % 2), 8)
            tiles = []
            for ring in range(RING):
                row = at // 4
                scale = spread(rows_held[part, ring, row : row + 1, :], at % 4)
                start = pl.multiple_of(128 * part, 128) + 16 * at
                tiles.append(x_held[ring, pl.ds(start, 8, stride=2), :] * scale)
            for ring, tile in enumerate(mix_bits(tiles, pick(chance, RING_HERE))):
                held[ring, plane, rows, :] = tile
        start_all([send(shift, part) for shift in range(RING)])

    @pl.loop(0, RING)
    def _(part):
        wait_all([send(shift, part) for shift in range(RING)])

    wait_all([send_rows(shift) for shift in range(RING)])


def begin_plane(rate_ref, class_ref, x_ref, out_ref, x_held, class_held, held, in_sems, out_sems, class_sem):
    chance = chances(rate_ref, 1)

    def load(ring):
        return pltpu.make_async_copy(x_ref.at[ring], x_held.at[ring], in_sems.at[ring])

    classes = pltpu.make_async_copy(class_ref, class_held, class_sem)
    classes.start()
    for ring in range(RING):
        load(ring).start()
    classes.wait()

    @pl.loop(0, RING)
    def _(ring):
        load(ring).wait()
        first_row = pl.multiple_of(REST * ring, REST)
        fitness = 0.5 + 0.25 * class_held[pl.ds(first_row, REST), :].astype(F32)
        for half in range(2):
            tiles = []
            for plane in range(PLANE):
                scale = spread(fitness[plane // 2 : plane // 2 + 1], plane % 2 * 2 + half)
                tiles.append(x_held[ring, pl.ds(32 * plane + 16 * half + 1, 8, stride=2), :] * scale)
            for plane, tile in enumerate(mix_bits(tiles, pick(chance, PLANE_HERE))):
                held[ring, plane, pl.ds(8 * half, 8), :] = tile
        plane_copy(out_ref, held, ring, out_sems, outward=True).start()

    wait_all([plane_copy(out_ref, held, ring, out_sems, outward=True) for ring in range(RING)])


def ring_to_plane_first(rate_ref, *refs):
    parts, out_ref, (held, rows_held, in_sems, out_sems, row_sem) = refs[:RING], refs[RING], refs[RING + 1 :]
    chance = chances(rate_ref, 0)
    copies = from_ring(parts, held, in_sems)()
    start_all(copies)
    wait_all(copies)
    for ring in range(RING):
        straight = held[ring, PLANE]
        turned = pltpu.roll(straight, 64, 1)
        for pair in range(REST):
            rows_held[2 * pair, ring : ring + 1, :] = straight[pair : pair + 1]
            rows_held[2 * pair + 1, ring : ring + 1, :] = turned[pair : pair + 1]
    rows_copy = pltpu.make_async_copy(rows_held, out_ref.at[:, pl.ds(RING * REST, RING), :], row_sem)
    rows_copy.start()
    mix_ring(held, pick(chance, RING_AWAY))

    def send(ring):
        return plane_copy(out_ref, held.at[:, pl.ds(0, PLANE)], ring, out_sems, outward=True)

    @pl.loop(0, RING)
    def _(ring):
        mix_plane(held, ring, pick(chance, PLANE_HERE))
        send(ring).start()

    wait_all([send(ring) for ring in range(RING)])
    rows_copy.wait()


TOGETHER = 4


def apply_middle(held, rows_held, first_ring, chance, left_ref, right_ref):
    left, right, across = left_ref[...], right_ref[...], chance[PLANE_AWAY[4]]
    rings = [first_ring + at for at in range(TOGETHER)]
    blocks = [held[ring].reshape(PLANE * REST, 128) for ring in rings]
    blocks = mix_blocks(blocks, left, right, across)
    scaled = []
    for ring, block in zip(rings, blocks):
        tiles = []
        for at in range(2 * PLANE):
            scale = spread(rows_held[at // 2, pl.ds(ring, 1), :], at % 2)
            tiles.append(block[8 * at : 8 * at + 8] * scale)
        scaled.append(jnp.concatenate(tiles, axis=0))
    blocks = mix_blocks(scaled, left, right, across)
    for ring, block in zip(rings, blocks):
        held[ring] = block.reshape(PLANE, REST, 128)


def middle_ring(rate_ref, x_ref, *refs):
    outs, (held, rows_held, left, right, in_sems, out_sems, row_sem) = refs[:RING], refs[RING:]
    chance = chances(rate_ref, 0)
    rows_copy = pltpu.make_async_copy(x_ref.at[:, pl.ds(RING * REST, RING), :], rows_held, row_sem)
    rows_copy.start()
    start_all([plane_copy(x_ref, held, ring, in_sems) for ring in range(RING)])
    left[...] = left_matrix(chance)
    right[...] = right_matrix(chance)
    rows_copy.wait()

    @pl.loop(0, RING, step=TOGETHER)
    def _(ring):
        for at in range(TOGETHER):
            plane_copy(x_ref, held, ring + at, in_sems).wait()
        apply_middle(held, rows_held, ring, chance, left, right)

    mix_ring(held, pick(chance, RING_AWAY), to_ring(held, outs, out_sems))


def ring_to_plane(rate_ref, *refs):
    parts, out_ref, (held, in_sems, out_sems) = refs[:RING], refs[RING], refs[RING + 1 :]
    chance = chances(rate_ref, 0)
    copies = from_ring(parts, held, in_sems)()
    start_all(copies)
    wait_all(copies)
    mix_ring(held, pick(chance, RING_HERE), to_plane(held, out_ref, out_sems))


def end_plane(rate_ref, x_ref, out_ref, held, in_sems, out_sems):
    chance = chances(rate_ref, 0)
    start_all([plane_copy(x_ref, held, ring, in_sems) for ring in range(RING)])

    def send(ring):
        return pltpu.make_async_copy(held.at[ring], out_ref.at[ring], out_sems.at[ring])

    @pl.loop(0, RING)
    def _(ring):
        plane_copy(x_ref, held, ring, in_sems).wait()
        mix_plane(held, ring, pick(chance, PLANE_HERE))
        send(ring).start()

    wait_all([send(ring) for ring in range(RING)])


def plane_to_ring_first(rate_ref, x_ref, *refs):
    outs, (held, in_sems, out_sems) = refs[:RING], refs[RING:]
    chance = chances(rate_ref, 1)
    copies = [plane_copy(x_ref, held, ring, in_sems) for ring in range(RING)]
    start_all(copies)
    wait_all(copies)
    mix_ring(held, pick(chance, RING_HERE), to_ring(held, outs, out_sems))


def plane_to_ring(rate_ref, x_ref, *refs):
    outs, (held, in_sems, out_sems) = refs[:RING], refs[RING:]
    chance = chances(rate_ref, 1)
    start_all([plane_copy(x_ref, held, ring, in_sems) for ring in range(RING)])

    def send(shift):
        return pltpu.make_async_copy(
            held.at[ring_slot(shift)], outs[shift], out_sems.at[shift, 0]
        )

    for shift in (3, 5, 2, 6, 1, 4, 7, 0):
        ring = ring_slot(shift)
        plane_copy(x_ref, held, ring, in_sems).wait()
        mix_plane(held, ring, pick(chance, PLANE_HERE))
        send(shift).start()
    wait_all([send(shift) for shift in range(RING)])


def middle_plane(rate_ref, fitness_ref, *refs):
    parts, out_ref, (held, rows_held, left, right, in_sems, out_sems, row_sem) = refs[:RING], refs[RING], refs[RING + 1 :]
    chance = chances(rate_ref, 1)
    rows_copy = pltpu.make_async_copy(fitness_ref.at[:, pl.ds(RING * REST, RING), :], rows_held, row_sem)
    rows_copy.start()
    copies = from_ring(parts, held, in_sems)()
    start_all(copies)
    left[...] = left_matrix(chance)
    right[...] = right_matrix(chance)
    rows_copy.wait()
    wait_all(copies)
    mix_ring(held, pick(chance, RING_AWAY))

    @pl.loop(0, RING, step=TOGETHER)
    def _(ring):
        apply_middle(held, rows_held, ring, chance, left, right)

    mix_ring(held, pick(chance, RING_AWAY), to_plane(held, out_ref, out_sems))


def end_ring(rate_ref, other_ref, *refs):
    parts, out_ref, (held, other_held, out_held, in_sems, other_sems, out_sems) = refs[:RING], refs[RING], refs[RING + 1 :]
    chance = chances(rate_ref, 1)
    other_copies = [
        pltpu.make_async_copy(other_ref.at[ring], other_held.at[ring], other_sems.at[ring])
        for ring in range(RING)
    ]
    copies = from_ring(parts, held, in_sems)()
    start_all(copies + other_copies)
    wait_all(copies + other_copies)

    def send(part):
        rows = pl.ds(pl.multiple_of(128 * part, 128), 128)
        return pltpu.make_async_copy(
            out_held.at[:, rows, :], out_ref.at[:, rows, :], out_sems.at[part]
        )

    @pl.loop(0, RING)
    def _(part):
        for at in range(8):
            plane, rows = 4 * part + at // 2, pl.ds(8 * (at % 2), 8)
            start = pl.multiple_of(128 * part + 16 * at, 16)
            tiles = [held[ring, plane, rows, :] for ring in range(RING)]
            for ring, tile in enumerate(mix_bits(tiles, pick(chance, RING_HERE))):
                out_held[ring, pl.ds(start, 8, stride=2), :] = other_held[ring, plane, rows, :]
                out_held[ring, pl.ds(start + 1, 8, stride=2), :] = tile
        send(part).start()

    wait_all([send(part) for part in range(RING)])


SMEM = pl.BlockSpec(memory_space=pltpu.SMEM)
ANY = pl.BlockSpec(memory_space=pl.ANY)
HELD = pltpu.VMEM((RING, PLANE, REST, 128), F32)
HELD_MORE = pltpu.VMEM((RING, PLANE + 1, REST, 128), F32)
WHOLE = pltpu.VMEM((RING, 1024, 128), F32)
CLASSES = pltpu.VMEM((128, 128), jnp.int32)
ROWS = pltpu.VMEM((PLANE, RING, 128), F32)
CLASS_ROWS = pltpu.VMEM((RING, RING, 8, 128), F32)
MANY = pltpu.SemaphoreType.DMA((RING, RING))
LEFT = pltpu.VMEM((256, 768), BF16)
RIGHT = pltpu.VMEM((256, 256), BF16)
EIGHT = pltpu.SemaphoreType.DMA((RING,))
ONE = pltpu.SemaphoreType.DMA
SENT_RING = [jax.ShapeDtypeStruct((PLANE, REST, 128), F32)] * RING
SENT_RING_MORE = [jax.ShapeDtypeStruct((PLANE + 1, REST, 128), F32)] * RING
SENT_PLANE = jax.ShapeDtypeStruct((PLANE, RING * REST, 128), F32)
SENT_PLANE_MORE = jax.ShapeDtypeStruct((PLANE, RING * REST + RING, 128), F32)


def far(shape):
    return pltpu.HBM(shape.shape, shape.dtype)


def call(kernel, name, outs, scratch, rate_index, *operands):
    many = isinstance(outs, list)
    return pl.pallas_call(
        kernel,
        out_shape=[far(out) for out in outs] if many else outs if name == "a5" else far(outs),
        in_specs=[SMEM] + [ANY] * len(operands),
        out_specs=[ANY] * len(outs) if many else ANY,
        scratch_shapes=scratch,
        cost_estimate=pl.CostEstimate(
            flops=1 << 28, bytes_accessed=8 << 20, transcendentals=0
        ),
        compiler_params=pltpu.CompilerParams(vmem_limit_bytes=(56 if name in ("a1", "b1") else 16) << 20),
    )(rate_index, *operands)


LATER = {"az1": (4, 6, 2, 7, 1), "bz1": (4, 6, 2, 7, 1), "az2": (4, 6, 2, 7, 1), "bz2": (6, 2, 7, 1)}


def sooner(name):
    return tuple(shift for shift in (3, 5, 4) if shift not in LATER[name])


def round_ring(parts, name):
    moved = list(parts)
    for shifts in (sooner(name), LATER[name]):
        for shift in shifts:
            moved[shift] = lax.ppermute(parts[shift], AXES, ring_pairs(shift))
    return moved


def in_plane(piece):
    return lax.all_to_all(
        piece, AXES, split_axis=0, concat_axis=0, tiled=True, axis_index_groups=PLANE_GROUPS
    )


def per_device(krylov, fitness_class, rate_index):
    rows = krylov.reshape(2, 4096, 128).transpose(1, 0, 2).reshape(RING, 1024, 128)
    classes = fitness_class.reshape(128, 128)
    rate = rate_index
    begin = [WHOLE, CLASSES]
    ends = [EIGHT, EIGHT]
    fine = [EIGHT, MANY]

    a = call(begin_ring, "a1", SENT_RING_MORE, begin + [HELD_MORE, CLASS_ROWS, EIGHT, MANY, ONE, EIGHT], rate, classes, rows)
    a = round_ring(a, "az1")
    b = call(begin_plane, "b1", SENT_PLANE, begin + [HELD] + ends + [ONE], rate, classes, rows)
    b = in_plane(b)
    b = call(plane_to_ring_first, "b2", SENT_RING, [HELD] + fine, rate, b)
    b = round_ring(b, "bz1")
    a = call(ring_to_plane_first, "a2", SENT_PLANE_MORE, [HELD_MORE, ROWS] + ends + [ONE], rate, *a)
    a = in_plane(a)
    fitness = a
    a = call(middle_ring, "a3", SENT_RING, [HELD, ROWS, LEFT, RIGHT] + fine + [ONE], rate, a)
    a = round_ring(a, "az2")
    b = call(middle_plane, "b3", SENT_PLANE, [HELD, ROWS, LEFT, RIGHT] + fine + [ONE], rate, fitness, *b)
    b = in_plane(b)
    b = call(plane_to_ring, "b4", SENT_RING, [HELD] + fine, rate, b)
    b = round_ring(b, "bz2")
    a = call(ring_to_plane, "a4", SENT_PLANE, [HELD] + fine, rate, *a)
    a = in_plane(a)
    done = jax.ShapeDtypeStruct((RING, PLANE, REST, 128), F32)
    a = call(end_plane, "a5", done, [HELD] + ends, rate, a)
    whole = jax.ShapeDtypeStruct((RING, 1024, 128), F32)
    result = call(end_ring, "b5", whole, [HELD, HELD, WHOLE, EIGHT] + ends, rate, a, *b)
    return result.reshape(4096, 2, 128).transpose(1, 0, 2).reshape(2, 4096 * 128)


def solution(mesh):
    in_specs = (P(None, AXES), P(AXES), P())
    out_specs = P(None, AXES)
    return jax.shard_map(per_device, mesh=mesh, in_specs=in_specs, out_specs=out_specs, check_vma=False)
```

```python
import jax
import jax.numpy as jnp
import numpy as np
from jax import lax
from jax.experimental import pallas as pl
from jax.experimental.pallas import tpu as pltpu
from jax.sharding import PartitionSpec as P


AXES = ("wide", "narrow")
SITES = 27
RING = 8
PLANE = 32
REST = 16
PROFILE = [float(1.0 + 0.5 * np.cos(2.0 * site)) for site in range(SITES)]
RING_HERE = [16, 17, 18]
PLANE_HERE = [11, 12, 13, 14, 15]
RING_AWAY = [25, 26, 21]
PLANE_AWAY = [19, 20, 22, 23, 24]
F32 = jnp.float32
BF16 = jnp.bfloat16


def device_at(ring, plane):
    x, core, y = plane // 8, plane // 4 % 2, plane % 4
    return ((ring % 4 * 4 + x) * 2 + core) * 8 + ring // 4 * 4 + y


def ring_pairs(shift):
    return [
        (device_at(ring, plane), device_at((ring + shift) % RING, plane))
        for ring in range(RING)
        for plane in range(PLANE)
    ]


PLANE_GROUPS = [[device_at(ring, plane) for plane in range(PLANE)] for ring in range(RING)]


def chances(rate_ref, vector):
    level = 0.004 * (rate_ref[vector].astype(F32) + 1.0)
    return [level * PROFILE[site] for site in range(SITES)]


def pick(chance, sites):
    return [chance[site] for site in sites]


def mix_bits(tiles, chance_of_bit):
    tiles = list(tiles)
    for bit, chance in enumerate(chance_of_bit):
        step = 1 << bit
        for low in range(len(tiles)):
            if low & step:
                continue
            flow = chance * (tiles[low | step] - tiles[low])
            tiles[low] = tiles[low] + flow
            tiles[low | step] = tiles[low | step] - flow
    return tiles


def crossing(size, chance_of_bit):
    row = lax.broadcasted_iota(jnp.int32, (size, size), 0)
    column = lax.broadcasted_iota(jnp.int32, (size, size), 1)
    differ = row ^ column
    product = jnp.ones((size, size), F32)
    for bit, chance in enumerate(chance_of_bit):
        product = product * jnp.where((differ >> bit) & 1 == 0, 1.0 - chance, chance)
    return halves(product)


def halves(values):
    high = values.astype(BF16)
    return high, (values - high.astype(F32)).astype(BF16)


def right_matrix(chance):
    high, low = crossing(128, chance[:7])
    top = jnp.concatenate([high, low], axis=1)
    bottom = jnp.concatenate([high, jnp.zeros_like(low)], axis=1)
    return jnp.concatenate([top, bottom], axis=0)


def left_matrix(chance):
    high, low = crossing(128, pick(chance, [7, 8, 9, 10] + PLANE_AWAY[:3]))
    return jnp.concatenate([high, high, low], axis=1)


def mix_blocks(blocks, left, right, chance):
    stacks = []
    for block in blocks:
        wide = jnp.concatenate([block[128 * at : 128 * at + 128] for at in range(4)], axis=1)
        high, low = halves(wide)
        stacks.append(jnp.concatenate([high, low, high], axis=0))
    mixed = [jnp.dot(left, stack, preferred_element_type=F32) for stack in stacks]
    pairs = []
    for both in mixed:
        quarters = mix_bits([both[:, 128 * at : 128 * at + 128] for at in range(4)], chance)
        pairs.append(jnp.concatenate(halves(jnp.concatenate(quarters, axis=0)), axis=1))
    mixed = [jnp.dot(pair, right, preferred_element_type=F32) for pair in pairs]
    return [both[:, :128] + both[:, 128:] for both in mixed]


def spread(row, pattern):
    sub = lax.broadcasted_iota(jnp.int32, (8, 128), 0)
    lane = lax.broadcasted_iota(jnp.int32, (8, 128), 1)
    index = 4 * (8 * pattern + sub) + (lane >> 5)
    return jnp.take_along_axis(
        jnp.broadcast_to(row, (8, 128)), index, axis=1, mode="promise_in_bounds"
    )


PARTS = 4
PART = PLANE // PARTS


def mix_ring(held, chance, sends=None):
    @pl.loop(0, PARTS)
    def _(part):
        for at in range(PART):
            for half in range(2):
                plane, rows = PART * part + at, pl.ds(8 * half, 8)
                mixed = mix_bits([held[ring, plane, rows, :] for ring in range(RING)], chance)
                for ring in range(RING):
                    held[ring, plane, rows, :] = mixed[ring]
        if sends:
            start_all(sends(part))

    if sends:

        @pl.loop(0, PARTS)
        def _(part):
            wait_all(sends(part))


def mix_plane(held, ring, chance):
    for half in range(2):
        rows = pl.ds(8 * half, 8)
        mixed = mix_bits([held[ring, plane, rows, :] for plane in range(PLANE)], chance)
        for plane in range(PLANE):
            held[ring, plane, rows, :] = mixed[plane]


def my_ring():
    return lax.axis_index("narrow") // 4 * 4 + lax.axis_index("wide") // 8


def ring_slot(shift):
    return lax.rem(my_ring() + shift + RING, RING)


def from_ring(refs, held, sems):
    def copies():
        return [
            pltpu.make_async_copy(ref, held.at[ring_slot(-shift)], sems.at[shift])
            for shift, ref in enumerate(refs)
        ]

    return copies


def to_ring(held, refs, sems):
    def copies(part):
        planes = pl.ds(PART * part, PART)
        return [
            pltpu.make_async_copy(
                held.at[ring_slot(shift), planes], ref.at[planes], sems.at[shift, part]
            )
            for shift, ref in enumerate(refs)
        ]

    return copies


def to_plane(held, ref, sems):
    def copies(part):
        planes = pl.ds(PART * part, PART)
        return [
            pltpu.make_async_copy(
                held.at[ring, planes],
                ref.at[planes, pl.ds(REST * ring, REST), :],
                sems.at[ring, part],
            )
            for ring in range(RING)
        ]

    return copies


def plane_copy(ref, held, ring, sems, outward=False):
    rows = pl.ds(pl.multiple_of(REST * ring, REST), REST)
    here, there = held.at[ring], ref.at[:, rows, :]
    if outward:
        return pltpu.make_async_copy(here, there, sems.at[ring])
    return pltpu.make_async_copy(there, here, sems.at[ring])


def start_all(copies):
    for copy in copies:
        copy.start()


def wait_all(copies):
    for copy in copies:
        copy.wait()


def begin_ring(rate_ref, class_ref, x_ref, *refs):
    outs, (x_held, class_held, held, rows_held, in_sems, out_sems, class_sem, rows_sems) = refs[:RING], refs[RING:]
    chance = chances(rate_ref, 0)

    def load(part):
        rows = pl.ds(pl.multiple_of(128 * part, 128), 128)
        return pltpu.make_async_copy(
            x_ref.at[:, rows, :], x_held.at[:, rows, :], in_sems.at[part]
        )

    def send(shift, part):
        planes = pl.ds(4 * part, 4)
        return pltpu.make_async_copy(
            held.at[ring_slot(shift), planes], outs[shift].at[planes], out_sems.at[shift, part]
        )

    def send_rows(shift):
        return pltpu.make_async_copy(
            held.at[ring_slot(shift), PLANE], outs[shift].at[PLANE], rows_sems.at[shift]
        )

    classes = pltpu.make_async_copy(class_ref, class_held, class_sem)
    classes.start()
    for part in range(RING):
        load(part).start()
    classes.wait()
    for ring in range(RING):
        fitness = 0.5 + 0.25 * class_held[REST * ring : REST * ring + REST].astype(F32)
        held[ring, PLANE] = fitness
        for part in range(RING):
            rows_held[part, ring, 0:2, :] = fitness[2 * part : 2 * part + 2]
    start_all([send_rows(shift) for shift in range(RING)])

    @pl.loop(0, RING)
    def _(part):
        load(part).wait()
        for at in range(8):
            plane, rows = 4 * part + at // 2, pl.ds(8 * (at % 2), 8)
            tiles = []
            for ring in range(RING):
                row = at // 4
                scale = spread(rows_held[part, ring, row : row + 1, :], at % 4)
                start = pl.multiple_of(128 * part, 128) + 16 * at
                tiles.append(x_held[ring, pl.ds(start, 8, stride=2), :] * scale)
            for ring, tile in enumerate(mix_bits(tiles, pick(chance, RING_HERE))):
                held[ring, plane, rows, :] = tile
        start_all([send(shift, part) for shift in range(RING)])

    @pl.loop(0, RING)
    def _(part):
        wait_all([send(shift, part) for shift in range(RING)])

    wait_all([send_rows(shift) for shift in range(RING)])


def begin_plane(rate_ref, class_ref, x_ref, out_ref, x_held, class_held, held, in_sems, out_sems, class_sem):
    chance = chances(rate_ref, 1)

    def load(ring):
        return pltpu.make_async_copy(x_ref.at[ring], x_held.at[ring], in_sems.at[ring])

    classes = pltpu.make_async_copy(class_ref, class_held, class_sem)
    classes.start()
    for ring in range(RING):
        load(ring).start()
    classes.wait()

    @pl.loop(0, RING)
    def _(ring):
        load(ring).wait()
        first_row = pl.multiple_of(REST * ring, REST)
        fitness = 0.5 + 0.25 * class_held[pl.ds(first_row, REST), :].astype(F32)
        for half in range(2):
            tiles = []
            for plane in range(PLANE):
                scale = spread(fitness[plane // 2 : plane // 2 + 1], plane % 2 * 2 + half)
                tiles.append(x_held[ring, pl.ds(32 * plane + 16 * half + 1, 8, stride=2), :] * scale)
            for plane, tile in enumerate(mix_bits(tiles, pick(chance, PLANE_HERE))):
                held[ring, plane, pl.ds(8 * half, 8), :] = tile
        plane_copy(out_ref, held, ring, out_sems, outward=True).start()

    wait_all([plane_copy(out_ref, held, ring, out_sems, outward=True) for ring in range(RING)])


def ring_to_plane_first(rate_ref, *refs):
    parts, out_ref, (held, rows_held, in_sems, out_sems, row_sem) = refs[:RING], refs[RING], refs[RING + 1 :]
    chance = chances(rate_ref, 0)
    copies = from_ring(parts, held, in_sems)()
    start_all(copies)
    wait_all(copies)
    for ring in range(RING):
        straight = held[ring, PLANE]
        turned = pltpu.roll(straight, 64, 1)
        for pair in range(REST):
            rows_held[2 * pair, ring : ring + 1, :] = straight[pair : pair + 1]
            rows_held[2 * pair + 1, ring : ring + 1, :] = turned[pair : pair + 1]
    rows_copy = pltpu.make_async_copy(rows_held, out_ref.at[:, pl.ds(RING * REST, RING), :], row_sem)
    rows_copy.start()
    mix_ring(held, pick(chance, RING_AWAY))

    def send(ring):
        return plane_copy(out_ref, held.at[:, pl.ds(0, PLANE)], ring, out_sems, outward=True)

    @pl.loop(0, RING)
    def _(ring):
        mix_plane(held, ring, pick(chance, PLANE_HERE))
        send(ring).start()

    wait_all([send(ring) for ring in range(RING)])
    rows_copy.wait()


TOGETHER = 8


def apply_middle(held, rows_held, first_ring, chance, left_ref, right_ref):
    left, right, across = left_ref[...], right_ref[...], pick(chance, PLANE_AWAY[3:])
    rings = [first_ring + at for at in range(TOGETHER)]
    blocks = [held[ring].reshape(PLANE * REST, 128) for ring in rings]
    blocks = mix_blocks(blocks, left, right, across)
    scaled = []
    for ring, block in zip(rings, blocks):
        tiles = []
        for at in range(2 * PLANE):
            scale = spread(rows_held[at // 2, pl.ds(ring, 1), :], at % 2)
            tiles.append(block[8 * at : 8 * at + 8] * scale)
        scaled.append(jnp.concatenate(tiles, axis=0))
    blocks = mix_blocks(scaled, left, right, across)
    for ring, block in zip(rings, blocks):
        held[ring] = block.reshape(PLANE, REST, 128)


def middle_ring(rate_ref, x_ref, *refs):
    outs, (held, rows_held, left, right, in_sems, out_sems, row_sem) = refs[:RING], refs[RING:]
    chance = chances(rate_ref, 0)
    rows_copy = pltpu.make_async_copy(x_ref.at[:, pl.ds(RING * REST, RING), :], rows_held, row_sem)
    rows_copy.start()
    start_all([plane_copy(x_ref, held, ring, in_sems) for ring in range(RING)])
    left[...] = left_matrix(chance)
    right[...] = right_matrix(chance)
    rows_copy.wait()

    @pl.loop(0, RING, step=TOGETHER)
    def _(ring):
        for at in range(TOGETHER):
            plane_copy(x_ref, held, ring + at, in_sems).wait()
        apply_middle(held, rows_held, ring, chance, left, right)

    mix_ring(held, pick(chance, RING_AWAY), to_ring(held, outs, out_sems))


def ring_to_plane(rate_ref, *refs):
    parts, out_ref, (held, in_sems, out_sems) = refs[:RING], refs[RING], refs[RING + 1 :]
    chance = chances(rate_ref, 0)
    copies = from_ring(parts, held, in_sems)()
    start_all(copies)
    wait_all(copies)
    mix_ring(held, pick(chance, RING_HERE), to_plane(held, out_ref, out_sems))


def end_plane(rate_ref, x_ref, out_ref, held, in_sems, out_sems):
    chance = chances(rate_ref, 0)
    start_all([plane_copy(x_ref, held, ring, in_sems) for ring in range(RING)])

    def send(ring):
        return pltpu.make_async_copy(held.at[ring], out_ref.at[ring], out_sems.at[ring])

    @pl.loop(0, RING)
    def _(ring):
        plane_copy(x_ref, held, ring, in_sems).wait()
        mix_plane(held, ring, pick(chance, PLANE_HERE))
        send(ring).start()

    wait_all([send(ring) for ring in range(RING)])


def plane_to_ring_first(rate_ref, x_ref, *refs):
    outs, (held, in_sems, out_sems) = refs[:RING], refs[RING:]
    chance = chances(rate_ref, 1)
    copies = [plane_copy(x_ref, held, ring, in_sems) for ring in range(RING)]
    start_all(copies)
    wait_all(copies)
    mix_ring(held, pick(chance, RING_HERE), to_ring(held, outs, out_sems))


def plane_to_ring(rate_ref, x_ref, *refs):
    outs, (held, in_sems, out_sems) = refs[:RING], refs[RING:]
    chance = chances(rate_ref, 1)
    start_all([plane_copy(x_ref, held, ring, in_sems) for ring in range(RING)])

    def send(shift):
        return pltpu.make_async_copy(
            held.at[ring_slot(shift)], outs[shift], out_sems.at[shift, 0]
        )

    for shift in (3, 5, 2, 6, 1, 4, 7, 0):
        ring = ring_slot(shift)
        plane_copy(x_ref, held, ring, in_sems).wait()
        mix_plane(held, ring, pick(chance, PLANE_HERE))
        send(shift).start()
    wait_all([send(shift) for shift in range(RING)])


def middle_plane(rate_ref, fitness_ref, *refs):
    parts, out_ref, (held, rows_held, left, right, in_sems, out_sems, row_sem) = refs[:RING], refs[RING], refs[RING + 1 :]
    chance = chances(rate_ref, 1)
    rows_copy = pltpu.make_async_copy(fitness_ref.at[:, pl.ds(RING * REST, RING), :], rows_held, row_sem)
    rows_copy.start()
    copies = from_ring(parts, held, in_sems)()
    start_all(copies)
    left[...] = left_matrix(chance)
    right[...] = right_matrix(chance)
    rows_copy.wait()
    wait_all(copies)
    mix_ring(held, pick(chance, RING_AWAY))

    @pl.loop(0, RING, step=TOGETHER)
    def _(ring):
        apply_middle(held, rows_held, ring, chance, left, right)

    mix_ring(held, pick(chance, RING_AWAY), to_plane(held, out_ref, out_sems))


def end_ring(rate_ref, other_ref, *refs):
    parts, out_ref, (held, other_held, out_held, in_sems, other_sems, out_sems) = refs[:RING], refs[RING], refs[RING + 1 :]
    chance = chances(rate_ref, 1)
    other_copies = [
        pltpu.make_async_copy(other_ref.at[ring], other_held.at[ring], other_sems.at[ring])
        for ring in range(RING)
    ]
    copies = from_ring(parts, held, in_sems)()
    start_all(copies + other_copies)
    wait_all(copies + other_copies)

    def send(part):
        rows = pl.ds(pl.multiple_of(128 * part, 128), 128)
        return pltpu.make_async_copy(
            out_held.at[:, rows, :], out_ref.at[:, rows, :], out_sems.at[part]
        )

    @pl.loop(0, RING)
    def _(part):
        for at in range(8):
            plane, rows = 4 * part + at // 2, pl.ds(8 * (at % 2), 8)
            start = pl.multiple_of(128 * part + 16 * at, 16)
            tiles = [held[ring, plane, rows, :] for ring in range(RING)]
            for ring, tile in enumerate(mix_bits(tiles, pick(chance, RING_HERE))):
                out_held[ring, pl.ds(start, 8, stride=2), :] = other_held[ring, plane, rows, :]
                out_held[ring, pl.ds(start + 1, 8, stride=2), :] = tile
        send(part).start()

    wait_all([send(part) for part in range(RING)])


SMEM = pl.BlockSpec(memory_space=pltpu.SMEM)
ANY = pl.BlockSpec(memory_space=pl.ANY)
HELD = pltpu.VMEM((RING, PLANE, REST, 128), F32)
HELD_MORE = pltpu.VMEM((RING, PLANE + 1, REST, 128), F32)
WHOLE = pltpu.VMEM((RING, 1024, 128), F32)
CLASSES = pltpu.VMEM((128, 128), jnp.int32)
ROWS = pltpu.VMEM((PLANE, RING, 128), F32)
CLASS_ROWS = pltpu.VMEM((RING, RING, 8, 128), F32)
MANY = pltpu.SemaphoreType.DMA((RING, RING))
LEFT = pltpu.VMEM((128, 384), BF16)
RIGHT = pltpu.VMEM((256, 256), BF16)
EIGHT = pltpu.SemaphoreType.DMA((RING,))
ONE = pltpu.SemaphoreType.DMA
SENT_RING = [jax.ShapeDtypeStruct((PLANE, REST, 128), F32)] * RING
SENT_RING_MORE = [jax.ShapeDtypeStruct((PLANE + 1, REST, 128), F32)] * RING
SENT_PLANE = jax.ShapeDtypeStruct((PLANE, RING * REST, 128), F32)
SENT_PLANE_MORE = jax.ShapeDtypeStruct((PLANE, RING * REST + RING, 128), F32)


def far(shape):
    return pltpu.HBM(shape.shape, shape.dtype)


def call(kernel, name, outs, scratch, rate_index, *operands):
    many = isinstance(outs, list)
    return pl.pallas_call(
        kernel,
        out_shape=[far(out) for out in outs] if many else outs if name == "a5" else far(outs),
        in_specs=[SMEM] + [ANY] * len(operands),
        out_specs=[ANY] * len(outs) if many else ANY,
        scratch_shapes=scratch,
        cost_estimate=pl.CostEstimate(
            flops=1 << 28, bytes_accessed=8 << 20, transcendentals=0
        ),
        compiler_params=pltpu.CompilerParams(vmem_limit_bytes=(56 if name in ("a1", "b1") else 16) << 20),
    )(rate_index, *operands)


LATER = {"az1": (2, 6, 4, 7, 1), "bz1": (2, 6, 4, 7, 1), "az2": (2, 6, 4, 7, 1), "bz2": (2, 6, 7, 1)}


def sooner(name):
    return tuple(shift for shift in (3, 5, 4) if shift not in LATER[name])


def round_ring(parts, name):
    moved = list(parts)
    for shifts in (sooner(name), LATER[name]):
        for shift in shifts:
            moved[shift] = lax.ppermute(parts[shift], AXES, ring_pairs(shift))
    return moved


def in_plane(piece):
    return lax.all_to_all(
        piece, AXES, split_axis=0, concat_axis=0, tiled=True, axis_index_groups=PLANE_GROUPS
    )


def per_device(krylov, fitness_class, rate_index):
    rows = krylov.reshape(2, 4096, 128).transpose(1, 0, 2).reshape(RING, 1024, 128)
    classes = fitness_class.reshape(128, 128)
    rate = rate_index
    begin = [WHOLE, CLASSES]
    ends = [EIGHT, EIGHT]
    fine = [EIGHT, MANY]

    a = call(begin_ring, "a1", SENT_RING_MORE, begin + [HELD_MORE, CLASS_ROWS, EIGHT, MANY, ONE, EIGHT], rate, classes, rows)
    a = round_ring(a, "az1")
    b = call(begin_plane, "b1", SENT_PLANE, begin + [HELD] + ends + [ONE], rate, classes, rows)
    b = in_plane(b)
    b = call(plane_to_ring_first, "b2", SENT_RING, [HELD] + fine, rate, b)
    b = round_ring(b, "bz1")
    a = call(ring_to_plane_first, "a2", SENT_PLANE_MORE, [HELD_MORE, ROWS] + ends + [ONE], rate, *a)
    a = in_plane(a)
    fitness = a
    a = call(middle_ring, "a3", SENT_RING, [HELD, ROWS, LEFT, RIGHT] + fine + [ONE], rate, a)
    a = round_ring(a, "az2")
    b = call(middle_plane, "b3", SENT_PLANE, [HELD, ROWS, LEFT, RIGHT] + fine + [ONE], rate, fitness, *b)
    b = in_plane(b)
    b = call(plane_to_ring, "b4", SENT_RING, [HELD] + fine, rate, b)
    b = round_ring(b, "bz2")
    a = call(ring_to_plane, "a4", SENT_PLANE, [HELD] + fine, rate, *a)
    a = in_plane(a)
    done = jax.ShapeDtypeStruct((RING, PLANE, REST, 128), F32)
    a = call(end_plane, "a5", done, [HELD] + ends, rate, a)
    whole = jax.ShapeDtypeStruct((RING, 1024, 128), F32)
    result = call(end_ring, "b5", whole, [HELD, HELD, WHOLE, EIGHT] + ends, rate, a, *b)
    return result.reshape(4096, 2, 128).transpose(1, 0, 2).reshape(2, 4096 * 128)


def solution(mesh):
    in_specs = (P(None, AXES), P(AXES), P())
    out_specs = P(None, AXES)
    return jax.shard_map(per_device, mesh=mesh, in_specs=in_specs, out_specs=out_specs, check_vma=False)
```
